32 devices in a mesh: grp: 1, lat: 32 (over z, y, x, core).
Axes of the slice: x: 2, y: 2, z: 4, core: 2. Of those that a mesh axis runs over, the one named last changes fastest.
Arguments:
- fields: bfloat16 [768, 64, 2048], P(('grp', 'lat')), may hold values from -6 to 6
- spectral_weight: bfloat16 [2, 128, 64, 128], replicated, may hold values from -0.5 to 0.5
- local_weight: bfloat16 [2, 64, 64], replicated, may hold values from -0.75 to 0.75
Outputs:
- updated: bfloat16 [768, 64, 2048], P(('grp', 'lat'))
The draws below stay inside these ranges and needn't reach their ends.
All inputs are finite; a program needn't handle non-finite values.
Results may differ from the reference program's by a relative error of at most 0.011.
Values may be sent and summed in bfloat16 or wider, within the bound.
A program may use at most 128 MiB of HBM per device.

```python
import math
import jax
import jax.numpy as jnp

C = 64
NLON = 2048
KX = 128
KY = 128
LAYERS = 2
ROWS_DEV = 24
NLAT = 768


def levels(stream_key, extent, split, low, largest):
    level = 1.0
    for position, shards_of in split:
        heights = jax.random.uniform(jax.random.fold_in(jax.random.fold_in(stream_key, 6), position), (shards_of,), jnp.float32, low / len(split), largest / len(split))
        level = level * jnp.repeat(jnp.exp(heights), extent[position] // shards_of).reshape((-1,) + (1,) * (len(extent) - 1 - position))
    return level


def centred(own_key, dims, spread, reach, split=(), kind=jnp.bfloat16):
    result = jax.random.normal(own_key, dims, jnp.float32) * spread
    if len(split) > 0:
        result = levels(own_key, dims, split, -0.22, 0.18) * result
    return jnp.clip(result, min=-reach, max=reach).astype(kind)


def setup_inputs(seed: int = 0, part: int = 0) -> dict:
    streams_of = jax.random.split(jax.random.key(seed), 4)
    part_keys = jax.random.split(jax.random.fold_in(streams_of[3], part), 4)
    fields = centred(part_keys[0], (NLAT, C, NLON), 1.0, 6.0, ((0, 32),))
    spectral_weight = centred(streams_of[1], (LAYERS, KX, C, 2 * C), (2 * C) ** -0.5, 0.5)
    local_weight = centred(streams_of[2], (LAYERS, C, C), C ** -0.5, 0.75)
    return {"fields": fields, "spectral_weight": spectral_weight, "local_weight": local_weight}


def lon_forward_table(lon_count, mode_count):
    cells = jnp.arange(lon_count, dtype=jnp.int32)[:, None]
    modes = jnp.arange(mode_count, dtype=jnp.int32)[None, :]
    angle = 2.0 * jnp.pi / lon_count * (cells * modes % lon_count).astype(jnp.float32)
    factor = 1.0 / math.sqrt(lon_count)
    return jnp.stack([jnp.cos(angle) * factor, -jnp.sin(angle) * factor], axis=1).astype(jnp.bfloat16)

def lon_back_table(lon_count, mode_count):
    modes = jnp.arange(mode_count, dtype=jnp.int32)[:, None]
    cells = jnp.arange(lon_count, dtype=jnp.int32)[None, :]
    angle = 2.0 * jnp.pi / lon_count * (cells * modes % lon_count).astype(jnp.float32)
    factor = 1.0 / math.sqrt(mode_count)
    return jnp.stack([jnp.cos(angle) * factor, -jnp.sin(angle) * factor], axis=1).astype(jnp.bfloat16)

def kept_wavenumbers(lat_count, kept_count):
    index = jnp.arange(kept_count, dtype=jnp.int32)
    return jnp.where(index < kept_count // 2, index, lat_count - kept_count + index).astype(jnp.int32)

def row_latitudes(lat_count, block_rows):
    rowids = jnp.arange(lat_count, dtype=jnp.int32)
    stride = lat_count // block_rows
    return (rowids % block_rows * stride + rowids // block_rows).astype(jnp.int32)

def lat_tables(lat_count, kept_count, block_rows):
    waves = kept_wavenumbers(lat_count, kept_count)
    latitudes = row_latitudes(lat_count, block_rows)
    angle = 2.0 * jnp.pi / lat_count * (waves[:, None] * latitudes[None, :] % lat_count).astype(jnp.float32)
    forward = jnp.stack([jnp.cos(angle), jnp.sin(angle)], axis=0) * (1.0 / math.sqrt(lat_count))
    backward = jnp.stack([jnp.cos(angle).T, jnp.sin(angle).T], axis=0) * (1.0 / math.sqrt(kept_count))
    return (forward.astype(jnp.bfloat16), backward.astype(jnp.bfloat16))

def lat_forward(table, values, channels):
    products = jnp.einsum('pjn,nkc->pjkc', table.astype(jnp.float32), values.astype(jnp.float32))
    real_part = products[0, ..., :channels] + products[1, ..., channels:]
    imag_part = products[0, ..., channels:] - products[1, ..., :channels]
    return jnp.concatenate([real_part, imag_part], axis=-1)

def lat_backward(table, modes, channels):
    products = jnp.einsum('pnj,jkc->pnkc', table.astype(jnp.float32), modes.astype(jnp.float32))
    real_part = products[0, ..., :channels] - products[1, ..., channels:]
    imag_part = products[1, ..., :channels] + products[0, ..., channels:]
    return jnp.concatenate([real_part, imag_part], axis=-1)

def mix_matrix(weight, channels):
    real_w = weight[..., :channels]
    imag_w = weight[..., channels:]
    lower = jnp.concatenate([-imag_w, real_w], axis=-1)
    return jnp.concatenate([weight, lower], axis=1)

def reference(fields, spectral_weight, local_weight):
    forward_lon = lon_forward_table(NLON, KX).astype(jnp.float32)
    backward_lon = lon_back_table(NLON, KX).astype(jnp.float32)
    forward_lat, backward_lat = lat_tables(NLAT, KY, ROWS_DEV)
    current = fields
    for layer_idx in range(LAYERS):
        wide = current.astype(jnp.float32)
        lon_modes = jnp.einsum('rcl,lpk->rkpc', wide, forward_lon)
        lon_modes = lon_modes.reshape(NLAT, KX, 2 * C).astype(jnp.bfloat16)
        lat_modes = lat_forward(forward_lat, lon_modes, C).astype(jnp.bfloat16)
        mixing = mix_matrix(spectral_weight[layer_idx], C).astype(jnp.float32)
        mixed_modes = jnp.einsum('jkc,kcd->jkd', lat_modes.astype(jnp.float32), mixing).astype(jnp.bfloat16)
        lat_back = lat_backward(backward_lat, mixed_modes, C).astype(jnp.bfloat16)
        spectral = jnp.einsum('rkpc,kpl->rcl', lat_back.reshape(NLAT, KX, 2, C).astype(jnp.float32), backward_lon)
        pointwise = jnp.einsum('rcl,cd->rdl', wide, local_weight[layer_idx].astype(jnp.float32))
        current = jax.nn.gelu(spectral + pointwise, approximate=True).astype(jnp.bfloat16)
    return current
```

```python
import functools
import math

import jax
import jax.numpy as jnp
import numpy as np
from jax import lax
from jax.experimental import pallas as pl
from jax.experimental.pallas import tpu as pltpu
from jax.sharding import PartitionSpec as P

KY = 128
MESH = pl.DeviceIdType.MESH
LAG = (0, 1, 4, 5, 8)
ROW_BLOCK = 8
CHUNK = 512


def lon_table(lon_count, mode_count):
    cells = np.arange(lon_count, dtype=np.int64)[:, None]
    modes = np.arange(mode_count, dtype=np.int64)[None, :]
    angle = (2.0 * np.pi / lon_count) * (cells * modes % lon_count)
    return np.stack([np.cos(angle), -np.sin(angle)], axis=1)


def lat_tables(devices, group, row_count, kept):
    lat_count = devices * row_count
    outer = devices // group
    index = np.arange(kept, dtype=np.int64)
    waves = np.where(index < kept // 2, index, lat_count - kept + index)
    plane = np.arange(outer)[:, None, None, None]
    row = np.arange(row_count).reshape(1, -1, 1, ROW_BLOCK)
    inner = np.arange(group)[None, None, :, None]
    latitudes = (row * devices + plane * group + inner).reshape(outer, -1)
    angle = (2.0 * np.pi / lat_count) * (waves[None, :, None] * latitudes[:, None, :] % lat_count)
    both = np.concatenate([np.cos(angle), np.sin(angle)], axis=2) / math.sqrt(lat_count)
    turned = angle.transpose(0, 2, 1)
    back = np.concatenate([np.cos(turned), -np.sin(turned)], axis=2) / math.sqrt(kept)
    return both, back


def modes_out(flat, turn):
    width = turn.shape[1]
    channels = width // 2
    rows = flat.shape[0] // channels
    modes = flat.shape[1] // 2
    for n in range(rows):
        part = flat[n * channels:(n + 1) * channels]
        stacked = jnp.concatenate([part[:, :modes], part[:, modes:]], axis=0)
        turn[pl.ds(n, modes, stride=rows), :] = stacked.T
    return turn[...].reshape(modes, rows, width).astype(jnp.bfloat16)


def block_mixing(local, pointwise):
    channels = local.shape[0]
    pointwise[...] = jnp.zeros_like(pointwise)
    mixing = (local.astype(jnp.float32).T * 0.5).astype(jnp.bfloat16)
    for n in range(pointwise.shape[0] // channels):
        own = slice(n * channels, (n + 1) * channels)
        pointwise[own, own] = mixing


def field_block(modes_in, h_ref, out_ref, back_ref, turn, turned, pointwise):
    modes, rows, width = modes_in.shape
    channels = width // 2
    lon_count = h_ref.shape[2]
    span = pointwise.shape[0] // channels
    turn[...] = modes_in.astype(jnp.float32).reshape(modes * rows, width)
    for n in range(rows):
        across = turn[pl.ds(n, modes, stride=rows), :].T
        turned[n * channels:(n + 1) * channels] = jnp.concatenate(
            [across[:channels], across[channels:]], axis=1
        ).astype(jnp.bfloat16)
    chunk = min(CHUNK, lon_count)
    inner = math.sqrt(2.0 / math.pi)
    for first in range(0, rows, span):
        many = span * channels
        spectrum = turned[first * channels:first * channels + many]
        for column in range(0, lon_count, chunk):
            cells = slice(column, column + chunk)
            half = jnp.dot(
                spectrum, back_ref[:, cells], preferred_element_type=jnp.float32
            ) + jnp.dot(
                pointwise[...], h_ref[first:first + span, :, cells].reshape(many, chunk),
                preferred_element_type=jnp.float32,
            )
            half = half.astype(jnp.bfloat16)
            curve = jnp.tanh(half * (2.0 * inner + (8.0 * inner * 0.044715) * (half * half)))
            out_ref[first:first + span, :, cells] = (
                (half * (1.0 + curve)).reshape(span, channels, chunk)
            )


def net_kernel(
    layers, group, outer, steps, order,
    h_ref, weight_ref, fwd_ref, bwd_ref, lon_ref, back_ref, local_ref, *rest,
):
    if layers > 1:
        y_ref, next_ref, *rest = rest
    else:
        y_ref, *rest = rest
    (
        h_buf, x_buf, r_buf, p_buf, q_buf, m_buf, v_buf, f_buf, acc,
        fwd_buf, bwd_buf, lon_buf, back_buf, w_buf, mix_buf, turn, turned, pointwise,
        h_sem, next_sem, table_sem, w_sem, own_in_sem, own_out_sem, f_sem, g_sem,
        a_send, a_recv, b_send, b_recv, c_send, c_recv, d_send, d_recv,
    ) = rest
    chunks, block, channels, lon_count = h_buf.shape
    modes, width = x_buf.shape[1], x_buf.shape[3]
    held = steps * outer
    kept = p_buf.shape[2]
    tall = chunks * group * block
    me = lax.axis_index("lat")
    z = me // group
    s = lax.rem(me, group)

    def inner_peer(i):
        return lax.rem(s + i, group)

    def outer_peer(i):
        return lax.rem(z + i, outer)

    h_copies = [
        pltpu.make_async_copy(h_ref.at[pl.ds(i * block, block)], h_buf.at[i], h_sem.at[i])
        for i in range(chunks)
    ]
    lon_copy = pltpu.make_async_copy(lon_ref, lon_buf, table_sem.at[0])
    back_copy = pltpu.make_async_copy(back_ref, back_buf, table_sem.at[1])
    fwd_copy = pltpu.make_async_copy(fwd_ref.at[z], fwd_buf, table_sem.at[2])
    bwd_copy = pltpu.make_async_copy(bwd_ref.at[z], bwd_buf, table_sem.at[3])
    w_copies = [
        pltpu.make_async_copy(
            weight_ref.at[l, (s * steps + t) * outer + z], w_buf.at[l, t], w_sem.at[l, t]
        )
        for l in range(layers) for t in range(steps)
    ]
    h_copies[0].start()
    lon_copy.start()
    for copy in h_copies[1:]:
        copy.start()

    barrier = pltpu.get_barrier_semaphore()
    for i in range(1, group):
        pl.semaphore_signal(
            barrier, inc=1, device_id={"lat": z * group + inner_peer(i)}, device_id_type=MESH
        )
    for i in range(1, outer):
        pl.semaphore_signal(
            barrier, inc=1, device_id={"lat": outer_peer(i) * group + s}, device_id_type=MESH
        )
    fwd_copy.start()
    bwd_copy.start()
    for copy in w_copies:
        copy.start()
    back_copy.start()

    parts = [(0, 1, 0, held)] if chunks > 1 else []
    first_tail = len(parts)
    parts += [(first_tail, chunks - first_tail, t * outer, outer) for t in range(steps)]

    def a_copy(part, i):
        to = inner_peer(i)
        c0, nc, m0, nm = parts[part]
        return pltpu.make_async_remote_copy(
            src_ref=x_buf.at[pl.ds(c0, nc), pl.ds(to * held + m0, nm)],
            dst_ref=r_buf.at[pl.ds(c0, nc), s, pl.ds(m0, nm)],
            send_sem=a_send.at[part, i], recv_sem=a_recv.at[part, i],
            device_id={"lat": z * group + to}, device_id_type=MESH,
        )

    def own_in(part):
        c0, nc, m0, nm = parts[part]
        return pltpu.make_async_copy(
            x_buf.at[pl.ds(c0, nc), pl.ds(s * held + m0, nm)],
            r_buf.at[pl.ds(c0, nc), s, pl.ds(m0, nm)],
            own_in_sem.at[part],
        )

    def b_copy(t, i):
        to = outer_peer(i)
        return pltpu.make_async_remote_copy(
            src_ref=p_buf.at[t, to], dst_ref=q_buf.at[t, z],
            send_sem=b_send.at[t, i], recv_sem=b_recv.at[t, i],
            device_id={"lat": to * group + s}, device_id_type=MESH,
        )

    def c_copy(t, i):
        to = outer_peer(i)
        return pltpu.make_async_remote_copy(
            src_ref=m_buf.at[t, z], dst_ref=m_buf.at[t, z],
            send_sem=c_send.at[t, i], recv_sem=c_recv.at[t, i],
            device_id={"lat": to * group + s}, device_id_type=MESH,
        )

    def d_copy(slot, c0, nc, t, i):
        to = inner_peer(i)
        return pltpu.make_async_remote_copy(
            src_ref=v_buf.at[pl.ds(c0, nc), to, pl.ds(t * outer, outer)],
            dst_ref=y_ref.at[pl.ds(c0, nc), pl.ds((s * steps + t) * outer, outer)],
            send_sem=d_send.at[slot, i], recv_sem=d_recv.at[slot, i],
            device_id={"lat": z * group + to}, device_id_type=MESH,
        )

    def own_out(slot, c0, nc, t):
        return pltpu.make_async_copy(
            v_buf.at[pl.ds(c0, nc), s, pl.ds(t * outer, outer)],
            y_ref.at[pl.ds(c0, nc), pl.ds((s * steps + t) * outer, outer)],
            own_out_sem.at[slot],
        )

    d_parts = [(t, 0, chunks, t) for t in range(steps - 1)]
    d_parts += [(steps - 1 + c, c, 1, steps - 1) for c in range(chunks)]

    def f_copy(t):
        return pltpu.make_async_remote_copy(
            src_ref=p_buf.at[t, outer - 1 - z], dst_ref=f_buf.at[t],
            send_sem=f_sem.at[0, t], recv_sem=f_sem.at[1, t],
            device_id={"lat": jnp.where(z == 0, 1, outer - 2) * group + s}, device_id_type=MESH,
        )

    def g_copy(t):
        block_of = outer_peer(2)
        return pltpu.make_async_remote_copy(
            src_ref=m_buf.at[t, block_of], dst_ref=m_buf.at[t, block_of],
            send_sem=g_sem.at[0, t], recv_sem=g_sem.at[1, t],
            device_id={"lat": (outer - 1 - block_of) * group + s}, device_id_type=MESH,
        )

    relay = outer == 4
    last = outer - 1
    at_end = jnp.logical_or(z == 0, z == last)
    inside = jnp.logical_not(at_end)
    lane = lax.broadcasted_iota(jnp.int32, (1, width), 1)
    sign = jnp.where(lane < channels, 1.0, -1.0)

    def swapped(values):
        return (pltpu.roll(values.astype(jnp.float32), channels, 1) * sign).astype(jnp.bfloat16)

    def lon_block(i):
        flat = jnp.dot(
            h_buf[i].reshape(block * channels, lon_count), lon_buf[...],
            preferred_element_type=jnp.float32,
        )
        x_buf[i] = modes_out(flat, turn)

    def send_part(part):
        own_in(part).start()
        for i in range(1, group):
            a_copy(part, i).start()

    def send_head(i):
        if first_tail:
            pl.when(i == 0)(lambda: send_part(0))

    def send_tail():
        for part in range(first_tail, len(parts)):
            send_part(part)

    def forward(t):
        for part in ([0] if t == 0 and first_tail else []) + [first_tail + t]:
            own_in(part).wait()
            for i in range(1, group):
                a_copy(part, i).wait_recv()
        for first in range(0, outer, 2):
            pair = []
            for u in range(first, min(first + 2, outer)):
                values = r_buf[:, :, t * outer + u].reshape(tall, width)
                pair.append(jnp.concatenate([values, swapped(values)], axis=0))
            out = jnp.dot(
                fwd_buf[...], jnp.concatenate(pair, axis=1), preferred_element_type=jnp.float32
            ).astype(jnp.bfloat16)
            for u in range(len(pair)):
                p_buf[t, first + u] = out[:, u * width:(u + 1) * width]
        if not relay:
            for i in range(1, outer):
                b_copy(t, i).start()
            return
        pl.when(at_end)(lambda: f_copy(t).start())
        pl.when(at_end)(lambda: b_copy(t, 2).start())
        pl.when(z != last)(lambda: b_copy(t, 1).start())
        pl.when(z != 0)(lambda: b_copy(t, last).start())

    def relay_sum(t):
        if not relay:
            return

        @pl.when(inside)
        def _():
            f_copy(t).wait_recv()
            to = outer_peer(2)
            p_buf[t, to] = (
                p_buf[t, to].astype(jnp.float32) + f_buf[t].astype(jnp.float32)
            ).astype(jnp.bfloat16)
            b_copy(t, 2).start()

    def collect(t, i):
        b_copy(t, i).wait_recv()
        acc[...] += q_buf[t, lax.rem(z + outer - i, outer)].astype(jnp.float32)

    def middle(t):
        acc[...] = p_buf[t, z].astype(jnp.float32)
        if relay:
            pl.when(z != 0)(lambda: collect(t, 1))
            pl.when(z != last)(lambda: collect(t, last))
            collect(t, 2)
        else:
            for i in range(1, outer):
                collect(t, i)
        mixed = jnp.dot(
            acc[...].astype(jnp.bfloat16), mix_buf[t], preferred_element_type=jnp.float32
        )
        m_buf[t, z] = mixed.astype(jnp.bfloat16)
        if relay:
            c_copy(t, 2).start()
            pl.when(z != last)(lambda: c_copy(t, 1).start())
            pl.when(z != 0)(lambda: c_copy(t, last).start())
        else:
            for i in range(1, outer):
                c_copy(t, i).start()

    def relay_out(t):
        if not relay:
            return

        @pl.when(inside)
        def _():
            c_copy(t, 2).wait_recv()
            g_copy(t).start()

    def backward(t):
        if relay:
            pl.when(z != 0)(lambda: c_copy(t, 1).wait_recv())
            pl.when(z != last)(lambda: c_copy(t, last).wait_recv())
            pl.when(at_end)(lambda: c_copy(t, 2).wait_recv())
            pl.when(at_end)(lambda: g_copy(t).wait_recv())
        else:
            for i in range(1, outer):
                c_copy(t, i).wait_recv()
        for first in range(0, outer, 2):
            pair = []
            for u in range(first, min(first + 2, outer)):
                values = m_buf[t, u]
                pair.append(jnp.concatenate([values, swapped(values)], axis=0))
            out = jnp.dot(
                bwd_buf[...], jnp.concatenate(pair, axis=1), preferred_element_type=jnp.float32
            ).astype(jnp.bfloat16)
            for u in range(len(pair)):
                v_buf[:, :, t * outer + first + u] = out[:, u * width:(u + 1) * width].reshape(
                    chunks, group, block, width
                )
        for slot, c0, nc, _ in [p for p in d_parts if p[3] == t]:
            for i in range(1, group):
                d_copy(slot, c0, nc, t, i).start()
            own_out(slot, c0, nc, t).start()

    def landed(slot, c0, nc, t):
        own_out(slot, c0, nc, t).wait()
        for i in range(1, group):
            d_copy(slot, c0, nc, t, i).wait_recv()

    def lat_sent():
        for part in range(len(parts)):
            for i in range(1, group):
                a_copy(part, i).wait_send()
        for t in range(steps):
            if relay:
                pl.when(at_end)(lambda: f_copy(t).wait_send())
                pl.when(inside)(lambda: g_copy(t).wait_send())
                for copy in (b_copy, c_copy):
                    copy(t, 2).wait_send()
                    pl.when(z != last)(lambda: copy(t, 1).wait_send())
                    pl.when(z != 0)(lambda: copy(t, last).wait_send())
            else:
                for i in range(1, outer):
                    b_copy(t, i).wait_send()
                    c_copy(t, i).wait_send()

    def back_sent():
        for slot, c0, nc, t in d_parts:
            for i in range(1, group):
                d_copy(slot, c0, nc, t, i).wait_send()

    stages = {
        "forward": forward, "relay_sum": relay_sum, "middle": middle,
        "relay_out": relay_out, "backward": backward,
    }

    def lat_block(layer):
        for t in range(steps):
            weight = w_buf[layer, t].astype(jnp.float32)
            mix_buf[t, :channels] = w_buf[layer, t]
            mix_buf[t, channels:] = (
                pltpu.roll(weight, channels, 1) * -sign
            ).astype(jnp.bfloat16)
        for name, t in order:
            stages[name](t)
        for part in d_parts[:steps - 1]:
            landed(*part)
        lat_sent()

    def next_copy(i):
        return pltpu.make_async_copy(
            h_buf.at[i], next_ref.at[pl.ds(i * block, block)], next_sem.at[i]
        )

    h_copies[0].wait()
    lon_copy.wait()

    @pl.loop(0, chunks)
    def _(i):
        lon_block(i)

        @pl.when(i == 0)
        def _():
            pl.semaphore_wait(barrier, group - 1 + outer - 1)
            for copy in h_copies[1:]:
                copy.wait()
        send_head(i)

    send_tail()
    fwd_copy.wait()
    bwd_copy.wait()
    for copy in w_copies:
        copy.wait()
    back_copy.wait()

    @pl.loop(0, layers)
    def _(layer):
        lat_block(layer)

        @pl.when(layer < layers - 1)
        def _():
            block_mixing(local_ref[layer], pointwise)

            @pl.loop(0, chunks)
            def _(i):
                landed(steps - 1 + i, i, 1, steps - 1)
                field_block(
                    y_ref[i], h_buf.at[i], h_buf.at[i], back_buf, turn, turned, pointwise
                )
                pl.when(layer == layers - 2)(lambda: next_copy(i).start())
                lon_block(i)
                send_head(i)

        @pl.when(layer == layers - 1)
        def _():
            for part in d_parts[steps - 1:]:
                landed(*part)
        back_sent()
        pl.when(layer < layers - 1)(send_tail)

    if layers > 1:
        for i in range(chunks):
            next_copy(i).wait()


def schedule(steps, lags):
    names = ("forward", "relay_sum", "middle", "relay_out", "backward")
    return [
        (name, step - lag)
        for step in range(steps + max(lags))
        for name, lag in zip(names, lags)
        if 0 <= step - lag < steps
    ]


def net_part(h, weight, fwd, bwd, lon, back, local, devices, group):
    rows, channels, lon_count = h.shape
    layers, modes, _, width = weight.shape
    outer = devices // group
    steps = modes // devices
    chunks = rows // ROW_BLOCK
    kept = fwd.shape[1]
    held = steps * outer
    dma = pltpu.SemaphoreType.DMA
    vmem = pl.BlockSpec(memory_space=pltpu.VMEM)
    hbm = pl.BlockSpec(memory_space=pl.ANY)
    bf16 = jnp.bfloat16
    many = max(1, min(ROW_BLOCK, 256 // channels)) * channels
    shapes = [jax.ShapeDtypeStruct((chunks, modes, ROW_BLOCK, width), bf16)]
    if layers > 1:
        shapes.append(jax.ShapeDtypeStruct(h.shape, bf16))
    part_count = steps + (1 if chunks > 1 else 0)
    slots = steps - 1 + chunks
    out = pl.pallas_call(
        functools.partial(net_kernel, layers, group, outer, steps, schedule(steps, LAG)),
        out_shape=shapes,
        in_specs=[hbm] * 6 + [vmem],
        out_specs=[vmem, hbm][:len(shapes)],
        scratch_shapes=[
            pltpu.VMEM((chunks, ROW_BLOCK, channels, lon_count), bf16),
            pltpu.VMEM((chunks, modes, ROW_BLOCK, width), bf16),
            pltpu.VMEM((chunks, group, held, ROW_BLOCK, width), bf16),
            pltpu.VMEM((steps, outer, kept, width), bf16),
            pltpu.VMEM((steps, outer, kept, width), bf16),
            pltpu.VMEM((steps, outer, kept, width), bf16),
            pltpu.VMEM((chunks, group, held, ROW_BLOCK, width), bf16),
            pltpu.VMEM((steps, kept, width), bf16),
            pltpu.VMEM((kept, width), jnp.float32),
            pltpu.VMEM(fwd.shape[1:], bf16),
            pltpu.VMEM(bwd.shape[1:], bf16),
            pltpu.VMEM(lon.shape, bf16),
            pltpu.VMEM(back.shape, bf16),
            pltpu.VMEM((layers, steps, channels, width), bf16),
            pltpu.VMEM((steps, width, width), bf16),
            pltpu.VMEM((modes * ROW_BLOCK, width), jnp.float32),
            pltpu.VMEM((ROW_BLOCK * channels, 2 * modes), bf16),
            pltpu.VMEM((many, many), bf16),
            dma((chunks,)), dma((chunks,)), dma((4,)), dma((layers, steps)),
            dma((part_count,)), dma((slots,)), dma((2, steps)), dma((2, steps)),
            dma((part_count, group)), dma((part_count, group)),
            dma((steps, outer)), dma((steps, outer)),
            dma((steps, outer)), dma((steps, outer)),
            dma((slots, group)), dma((slots, group)),
        ],
        compiler_params=pltpu.CompilerParams(collective_id=0, has_side_effects=True),
        name="net_part",
    )(h, weight, fwd, bwd, lon, back, local)
    return out[0], (out[1] if layers > 1 else h)


def field_kernel(layer, y_ref, h_ref, back_ref, local_ref, out_ref, turn, turned, pointwise):
    @pl.when(pl.program_id(0) == 0)
    def _():
        block_mixing(local_ref[layer], pointwise)

    field_block(y_ref[0], h_ref, out_ref, back_ref, turn, turned, pointwise)


def whole_block(array):
    return pl.BlockSpec(array.shape, lambda i: (0,) * array.ndim, pipeline_mode=pl.Buffered(1))


def field_part(y, h, back, local, layer):
    rows, channels, lon_count = h.shape
    _, modes, _, width = y.shape
    field = pl.BlockSpec((ROW_BLOCK, channels, lon_count), lambda i: (i, 0, 0))
    spectral = pl.BlockSpec((1, modes, ROW_BLOCK, width), lambda i: (i, 0, 0, 0))
    many = max(1, min(ROW_BLOCK, 256 // channels)) * channels
    return pl.pallas_call(
        functools.partial(field_kernel, layer),
        grid=(rows // ROW_BLOCK,),
        out_shape=jax.ShapeDtypeStruct(h.shape, jnp.bfloat16),
        in_specs=[spectral, field, whole_block(back), whole_block(local)],
        out_specs=field,
        scratch_shapes=[
            pltpu.VMEM((modes * ROW_BLOCK, width), jnp.float32),
            pltpu.VMEM((ROW_BLOCK * channels, 2 * modes), jnp.bfloat16),
            pltpu.VMEM((many, many), jnp.bfloat16),
        ],
        name="field_part",
    )(y, h, back, local)


def shards(fields, spectral_weight, local_weight):
    row_count, channels, lon_count = fields.shape
    layer_count, mode_rows = spectral_weight.shape[:2]
    devices = lax.axis_size("lat")
    group = math.gcd(devices, 8)
    table = lon_table(lon_count, mode_rows)
    forward_lon = jnp.asarray(
        (table / math.sqrt(lon_count)).reshape(lon_count, 2 * mode_rows), jnp.bfloat16
    )
    backward_lon = jnp.asarray(
        (table.transpose(1, 2, 0) * (0.5 / math.sqrt(mode_rows))).reshape(
            2 * mode_rows, lon_count
        ),
        jnp.bfloat16,
    )
    forward_all, backward_all = lat_tables(devices, group, row_count, KY)
    forward_lat = jnp.asarray(forward_all, jnp.bfloat16)
    backward_lat = jnp.asarray(backward_all, jnp.bfloat16)
    y, h = net_part(
        fields, spectral_weight, forward_lat, backward_lat, forward_lon, backward_lon,
        local_weight, devices, group,
    )
    return field_part(y, h, backward_lon, local_weight, layer_count - 1)


def solution(mesh):
    return jax.shard_map(
        shards,
        mesh=mesh,
        in_specs=(P(("grp", "lat"), None, None), P(), P()),
        out_specs=P(("grp", "lat"), None, None),
        check_vma=False,
    )
```

```python
import functools
import math

import jax
import jax.numpy as jnp
import numpy as np
from jax import lax
from jax.experimental import pallas as pl
from jax.experimental.pallas import tpu as pltpu
from jax.sharding import PartitionSpec as P

KY = 128
MESH = pl.DeviceIdType.MESH
LAG = (0, 1, 4, 5, 8)
ROW_BLOCK = 8
CHUNK = 512
NET_VMEM = 20 << 20
FIELD_VMEM = 8 << 20


def lon_table(lon_count, mode_count):
    cells = np.arange(lon_count, dtype=np.int64)[:, None]
    modes = np.arange(mode_count, dtype=np.int64)[None, :]
    angle = (2.0 * np.pi / lon_count) * (cells * modes % lon_count)
    return np.stack([np.cos(angle), -np.sin(angle)], axis=1)


def lat_tables(devices, group, row_count, kept):
    lat_count = devices * row_count
    outer = devices // group
    index = np.arange(kept, dtype=np.int64)
    waves = np.where(index < kept // 2, index, lat_count - kept + index)
    plane = np.arange(outer)[:, None, None, None]
    row = np.arange(row_count).reshape(1, -1, 1, ROW_BLOCK)
    inner = np.arange(group)[None, None, :, None]
    latitudes = (row * devices + plane * group + inner).reshape(outer, -1)
    angle = (2.0 * np.pi / lat_count) * (waves[None, :, None] * latitudes[:, None, :] % lat_count)
    both = np.concatenate([np.cos(angle), np.sin(angle)], axis=2) / math.sqrt(lat_count)
    turned = angle.transpose(0, 2, 1)
    back = np.concatenate([np.cos(turned), -np.sin(turned)], axis=2) / math.sqrt(kept)
    return both, back


def modes_out(flat, turn):
    width = turn.shape[1]
    channels = width // 2
    rows = flat.shape[0] // channels
    modes = flat.shape[1] // 2
    for n in range(rows):
        part = flat[n * channels:(n + 1) * channels]
        stacked = jnp.concatenate([part[:, :modes], part[:, modes:]], axis=0)
        turn[pl.ds(n, modes, stride=rows), :] = stacked.T
    return turn[...].reshape(modes, rows, width).astype(jnp.bfloat16)


def block_mixing(local, pointwise):
    channels = local.shape[0]
    pointwise[...] = jnp.zeros_like(pointwise)
    mixing = (local.astype(jnp.float32).T * 0.5).astype(jnp.bfloat16)
    for n in range(pointwise.shape[0] // channels):
        own = slice(n * channels, (n + 1) * channels)
        pointwise[own, own] = mixing


def pointwise_block(h_ref, out_ref, pointwise):
    rows, channels, lon_count = h_ref.shape
    many = pointwise.shape[0]
    span = many // channels
    chunk = min(CHUNK, lon_count)
    for first in range(0, rows, span):
        for column in range(0, lon_count, chunk):
            cells = slice(column, column + chunk)
            out_ref[first * channels:first * channels + many, cells] = jnp.dot(
                pointwise[...], h_ref[first:first + span, :, cells].reshape(many, chunk),
                preferred_element_type=jnp.float32,
            )


def spectrum_block(modes_in, turn, turned):
    modes, rows, width = modes_in.shape
    channels = width // 2
    turn[...] = modes_in.astype(jnp.float32).reshape(modes * rows, width)
    for n in range(rows):
        across = turn[pl.ds(n, modes, stride=rows), :].T
        turned[n * channels:(n + 1) * channels] = jnp.concatenate(
            [across[:channels], across[channels:]], axis=1
        ).astype(jnp.bfloat16)


def field_rows(first, span, local_ref, out_ref, back_ref, turned):
    _, channels, lon_count = out_ref.shape
    chunk = min(CHUNK, lon_count)
    inner = math.sqrt(2.0 / math.pi)
    own = slice(first * channels, (first + span) * channels)
    for column in range(0, lon_count, chunk):
        cells = slice(column, column + chunk)
        half = local_ref[own, cells] + jnp.dot(
            turned[own], back_ref[:, cells], preferred_element_type=jnp.float32
        )
        half = half.astype(jnp.bfloat16)
        curve = jnp.tanh(half * (2.0 * inner + (8.0 * inner * 0.044715) * (half * half)))
        out_ref[first:first + span, :, cells] = (
            (half * (1.0 + curve)).reshape(span, channels, chunk)
        )


def net_kernel(
    layers, group, outer, steps, order,
    h_ref, weight_ref, fwd_ref, bwd_ref, lon_ref, back_ref, mixing_ref, *rest,
):
    (
        y_ref, pw_buf, back_buf, h_buf, x_buf, r_buf, p_buf, q_buf, m_buf, v_buf, f_buf, acc,
        fwd_buf, bwd_buf, lon_buf, local_ref, w_buf, mix_buf, turn, turned, pointwise,
        h_sem, table_sem, w_sem, own_in_sem, own_out_sem, f_sem, g_sem,
        a_send, a_recv, b_send, b_recv, c_send, c_recv, d_send, d_recv,
    ) = rest
    span = pointwise.shape[0] // h_buf.shape[2]
    chunks, block, channels, lon_count = h_buf.shape
    modes, width = x_buf.shape[1], x_buf.shape[3]
    held = steps * outer
    kept = p_buf.shape[2]
    tall = chunks * group * block
    me = lax.axis_index("lat")
    z = me // group
    s = lax.rem(me, group)

    def inner_peer(i):
        return lax.rem(s + i, group)

    def outer_peer(i):
        return lax.rem(z + i, outer)

    h_copies = [
        pltpu.make_async_copy(h_ref.at[pl.ds(i * block, block)], h_buf.at[i], h_sem.at[i])
        for i in range(chunks)
    ]
    lon_copy = pltpu.make_async_copy(lon_ref, lon_buf, table_sem.at[0])
    local_copy = pltpu.make_async_copy(mixing_ref, local_ref, table_sem.at[4])
    back_copy = pltpu.make_async_copy(back_ref, back_buf, table_sem.at[1])
    fwd_copy = pltpu.make_async_copy(fwd_ref.at[z], fwd_buf, table_sem.at[2])
    bwd_copy = pltpu.make_async_copy(bwd_ref.at[z], bwd_buf, table_sem.at[3])
    w_copies = [
        pltpu.make_async_copy(
            weight_ref.at[l, (s * steps + t) * outer + z], w_buf.at[l, t], w_sem.at[l, t]
        )
        for l in range(layers) for t in range(steps)
    ]
    h_copies[0].start()
    lon_copy.start()
    for copy in h_copies[1:]:
        copy.start()

    barrier = pltpu.get_barrier_semaphore()
    for i in range(1, group):
        pl.semaphore_signal(
            barrier, inc=1, device_id={"lat": z * group + inner_peer(i)}, device_id_type=MESH
        )
    for i in range(1, outer):
        pl.semaphore_signal(
            barrier, inc=1, device_id={"lat": outer_peer(i) * group + s}, device_id_type=MESH
        )
    local_copy.start()
    fwd_copy.start()
    bwd_copy.start()
    for copy in w_copies:
        copy.start()
    back_copy.start()

    parts = [(0, 1, 0, held)] if chunks > 1 else []
    first_tail = len(parts)
    parts += [(first_tail, chunks - first_tail, t * outer, outer) for t in range(steps)]

    def a_copy(part, i):
        to = inner_peer(i)
        c0, nc, m0, nm = parts[part]
        return pltpu.make_async_remote_copy(
            src_ref=x_buf.at[pl.ds(c0, nc), pl.ds(to * held + m0, nm)],
            dst_ref=r_buf.at[pl.ds(c0, nc), s, pl.ds(m0, nm)],
            send_sem=a_send.at[part, i], recv_sem=a_recv.at[part, i],
            device_id={"lat": z * group + to}, device_id_type=MESH,
        )

    def own_in(part):
        c0, nc, m0, nm = parts[part]
        return pltpu.make_async_copy(
            x_buf.at[pl.ds(c0, nc), pl.ds(s * held + m0, nm)],
            r_buf.at[pl.ds(c0, nc), s, pl.ds(m0, nm)],
            own_in_sem.at[part],
        )

    def b_copy(t, i):
        to = outer_peer(i)
        return pltpu.make_async_remote_copy(
            src_ref=p_buf.at[t, to], dst_ref=q_buf.at[t, z],
            send_sem=b_send.at[t, i], recv_sem=b_recv.at[t, i],
            device_id={"lat": to * group + s}, device_id_type=MESH,
        )

    def c_copy(t, i):
        to = outer_peer(i)
        return pltpu.make_async_remote_copy(
            src_ref=m_buf.at[t, z], dst_ref=m_buf.at[t, z],
            send_sem=c_send.at[t, i], recv_sem=c_recv.at[t, i],
            device_id={"lat": to * group + s}, device_id_type=MESH,
        )

    def d_copy(slot, c0, nc, t, i):
        to = inner_peer(i)
        return pltpu.make_async_remote_copy(
            src_ref=v_buf.at[pl.ds(c0, nc), to, pl.ds(t * outer, outer)],
            dst_ref=y_ref.at[pl.ds(c0, nc), pl.ds((s * steps + t) * outer, outer)],
            send_sem=d_send.at[slot, i], recv_sem=d_recv.at[slot, i],
            device_id={"lat": z * group + to}, device_id_type=MESH,
        )

    def own_out(slot, c0, nc, t):
        return pltpu.make_async_copy(
            v_buf.at[pl.ds(c0, nc), s, pl.ds(t * outer, outer)],
            y_ref.at[pl.ds(c0, nc), pl.ds((s * steps + t) * outer, outer)],
            own_out_sem.at[slot],
        )

    d_parts = [(t, 0, chunks, t) for t in range(steps - 1)]
    d_parts += [(steps - 1 + c, c, 1, steps - 1) for c in range(chunks)]

    def f_copy(t):
        return pltpu.make_async_remote_copy(
            src_ref=p_buf.at[t, outer - 1 - z], dst_ref=f_buf.at[t],
            send_sem=f_sem.at[0, t], recv_sem=f_sem.at[1, t],
            device_id={"lat": jnp.where(z == 0, 1, outer - 2) * group + s}, device_id_type=MESH,
        )

    def g_copy(t):
        block_of = outer_peer(2)
        return pltpu.make_async_remote_copy(
            src_ref=m_buf.at[t, block_of], dst_ref=m_buf.at[t, block_of],
            send_sem=g_sem.at[0, t], recv_sem=g_sem.at[1, t],
            device_id={"lat": (outer - 1 - block_of) * group + s}, device_id_type=MESH,
        )

    relay = outer == 4
    last = outer - 1
    at_end = jnp.logical_or(z == 0, z == last)
    inside = jnp.logical_not(at_end)
    lane = lax.broadcasted_iota(jnp.int32, (1, width), 1)
    sign = jnp.where(lane < channels, 1.0, -1.0)

    def swapped(values):
        return (pltpu.roll(values.astype(jnp.float32), channels, 1) * sign).astype(jnp.bfloat16)

    def lon_block(i):
        flat = jnp.dot(
            h_buf[i].reshape(block * channels, lon_count), lon_buf[...],
            preferred_element_type=jnp.float32,
        )
        x_buf[i] = modes_out(flat, turn)

    def send_part(part):
        own_in(part).start()
        for i in range(1, group):
            a_copy(part, i).start()

    def send_head(i):
        if first_tail:
            pl.when(i == 0)(lambda: send_part(0))

    def send_tail():
        for part in range(first_tail, len(parts)):
            send_part(part)

    def forward(t):
        for part in ([0] if t == 0 and first_tail else []) + [first_tail + t]:
            own_in(part).wait()
            for i in range(1, group):
                a_copy(part, i).wait_recv()
        for first in range(0, outer, 2):
            pair = []
            for u in range(first, min(first + 2, outer)):
                values = r_buf[:, :, t * outer + u].reshape(tall, width)
                pair.append(jnp.concatenate([values, swapped(values)], axis=0))
            out = jnp.dot(
                fwd_buf[...], jnp.concatenate(pair, axis=1), preferred_element_type=jnp.float32
            ).astype(jnp.bfloat16)
            for u in range(len(pair)):
                p_buf[t, first + u] = out[:, u * width:(u + 1) * width]
        if not relay:
            for i in range(1, outer):
                b_copy(t, i).start()
            return
        pl.when(at_end)(lambda: f_copy(t).start())
        pl.when(at_end)(lambda: b_copy(t, 2).start())
        pl.when(z != last)(lambda: b_copy(t, 1).start())
        pl.when(z != 0)(lambda: b_copy(t, last).start())

    def relay_sum(t):
        if not relay:
            return

        @pl.when(inside)
        def _():
            f_copy(t).wait_recv()
            to = outer_peer(2)
            p_buf[t, to] = (
                p_buf[t, to].astype(jnp.float32) + f_buf[t].astype(jnp.float32)
            ).astype(jnp.bfloat16)
            b_copy(t, 2).start()

    def collect(t, i):
        b_copy(t, i).wait_recv()
        acc[...] += q_buf[t, lax.rem(z + outer - i, outer)].astype(jnp.float32)

    def middle(t):
        acc[...] = p_buf[t, z].astype(jnp.float32)
        if relay:
            pl.when(z != 0)(lambda: collect(t, 1))
            pl.when(z != last)(lambda: collect(t, last))
            collect(t, 2)
        else:
            for i in range(1, outer):
                collect(t, i)
        mixed = jnp.dot(
            acc[...].astype(jnp.bfloat16), mix_buf[t], preferred_element_type=jnp.float32
        )
        m_buf[t, z] = mixed.astype(jnp.bfloat16)
        if relay:
            c_copy(t, 2).start()
            pl.when(z != last)(lambda: c_copy(t, 1).start())
            pl.when(z != 0)(lambda: c_copy(t, last).start())
        else:
            for i in range(1, outer):
                c_copy(t, i).start()

    def relay_out(t):
        if not relay:
            return

        @pl.when(inside)
        def _():
            c_copy(t, 2).wait_recv()
            g_copy(t).start()

    def backward(t):
        if relay:
            pl.when(z != 0)(lambda: c_copy(t, 1).wait_recv())
            pl.when(z != last)(lambda: c_copy(t, last).wait_recv())
            pl.when(at_end)(lambda: c_copy(t, 2).wait_recv())
            pl.when(at_end)(lambda: g_copy(t).wait_recv())
        else:
            for i in range(1, outer):
                c_copy(t, i).wait_recv()
        for first in range(0, outer, 2):
            pair = []
            for u in range(first, min(first + 2, outer)):
                values = m_buf[t, u]
                pair.append(jnp.concatenate([values, swapped(values)], axis=0))
            out = jnp.dot(
                bwd_buf[...], jnp.concatenate(pair, axis=1), preferred_element_type=jnp.float32
            ).astype(jnp.bfloat16)
            for u in range(len(pair)):
                v_buf[:, :, t * outer + first + u] = out[:, u * width:(u + 1) * width].reshape(
                    chunks, group, block, width
                )
        for slot, c0, nc, _ in [p for p in d_parts if p[3] == t]:
            for i in range(1, group):
                d_copy(slot, c0, nc, t, i).start()
            own_out(slot, c0, nc, t).start()

    def landed(slot, c0, nc, t):
        own_out(slot, c0, nc, t).wait()
        for i in range(1, group):
            d_copy(slot, c0, nc, t, i).wait_recv()

    def lat_sent():
        for part in range(len(parts)):
            for i in range(1, group):
                a_copy(part, i).wait_send()
        for t in range(steps):
            if relay:
                pl.when(at_end)(lambda: f_copy(t).wait_send())
                pl.when(inside)(lambda: g_copy(t).wait_send())
                for copy in (b_copy, c_copy):
                    copy(t, 2).wait_send()
                    pl.when(z != last)(lambda: copy(t, 1).wait_send())
                    pl.when(z != 0)(lambda: copy(t, last).wait_send())
            else:
                for i in range(1, outer):
                    b_copy(t, i).wait_send()
                    c_copy(t, i).wait_send()

    def back_sent():
        for slot, c0, nc, t in d_parts:
            for i in range(1, group):
                d_copy(slot, c0, nc, t, i).wait_send()

    stages = {
        "forward": forward, "relay_sum": relay_sum, "middle": middle,
        "relay_out": relay_out, "backward": backward,
    }

    def lat_block(layer):
        for t in range(steps):
            weight = w_buf[layer, t].astype(jnp.float32)
            mix_buf[t, :channels] = w_buf[layer, t]
            mix_buf[t, channels:] = (
                pltpu.roll(weight, channels, 1) * -sign
            ).astype(jnp.bfloat16)
        block_mixing(local_ref[layer], pointwise)

        @pl.loop(0, chunks)
        def _(i):
            pointwise_block(h_buf.at[i], pw_buf.at[i], pointwise)

        for name, t in order:
            stages[name](t)
        for part in d_parts[:steps - 1]:
            landed(*part)
        lat_sent()

    h_copies[0].wait()
    lon_copy.wait()

    @pl.loop(0, chunks)
    def _(i):
        lon_block(i)

        @pl.when(i == 0)
        def _():
            pl.semaphore_wait(barrier, group - 1 + outer - 1)
            for copy in h_copies[1:]:
                copy.wait()
        send_head(i)

    send_tail()
    local_copy.wait()
    fwd_copy.wait()
    bwd_copy.wait()
    for copy in w_copies:
        copy.wait()
    back_copy.wait()

    @pl.loop(0, layers)
    def _(layer):
        lat_block(layer)

        @pl.when(layer < layers - 1)
        def _():
            @pl.loop(0, chunks)
            def _(i):
                landed(steps - 1 + i, i, 1, steps - 1)
                spectrum_block(y_ref[i], turn, turned)
                for first in range(0, block, span):
                    field_rows(first, span, pw_buf.at[i], h_buf.at[i], back_buf, turned)
                lon_block(i)
                send_head(i)

        @pl.when(layer == layers - 1)
        def _():
            for part in d_parts[steps - 1:]:
                landed(*part)
        back_sent()
        pl.when(layer < layers - 1)(send_tail)


def schedule(steps, lags):
    names = ("forward", "relay_sum", "middle", "relay_out", "backward")
    return [
        (name, step - lag)
        for step in range(steps + max(lags))
        for name, lag in zip(names, lags)
        if 0 <= step - lag < steps
    ]


def net_part(h, weight, fwd, bwd, lon, back, local, devices, group):
    rows, channels, lon_count = h.shape
    layers, modes, _, width = weight.shape
    outer = devices // group
    steps = modes // devices
    chunks = rows // ROW_BLOCK
    kept = fwd.shape[1]
    held = steps * outer
    dma = pltpu.SemaphoreType.DMA
    vmem = pl.BlockSpec(memory_space=pltpu.VMEM)
    hbm = pl.BlockSpec(memory_space=pltpu.HBM)
    bf16 = jnp.bfloat16
    many = max(1, min(ROW_BLOCK, 256 // channels)) * channels
    shapes = [
        jax.ShapeDtypeStruct((chunks, modes, ROW_BLOCK, width), bf16),
        jax.ShapeDtypeStruct((chunks, ROW_BLOCK * channels, lon_count), jnp.float32),
        jax.ShapeDtypeStruct(back.shape, bf16),
    ]
    part_count = steps + (1 if chunks > 1 else 0)
    slots = steps - 1 + chunks
    operands = [
        pltpu.with_memory_space_constraint(a, pltpu.HBM)
        for a in (h, weight, fwd, bwd, lon, back, local)
    ]
    return pl.pallas_call(
        functools.partial(net_kernel, layers, group, outer, steps, schedule(steps, LAG)),
        out_shape=shapes,
        in_specs=[hbm] * 7,
        out_specs=[vmem] * 3,
        scratch_shapes=[
            pltpu.VMEM((chunks, ROW_BLOCK, channels, lon_count), bf16),
            pltpu.VMEM((chunks, modes, ROW_BLOCK, width), bf16),
            pltpu.VMEM((chunks, group, held, ROW_BLOCK, width), bf16),
            pltpu.VMEM((steps, outer, kept, width), bf16),
            pltpu.VMEM((steps, outer, kept, width), bf16),
            pltpu.VMEM((steps, outer, kept, width), bf16),
            pltpu.VMEM((chunks, group, held, ROW_BLOCK, width), bf16),
            pltpu.VMEM((steps, kept, width), bf16),
            pltpu.VMEM((kept, width), jnp.float32),
            pltpu.VMEM(fwd.shape[1:], bf16),
            pltpu.VMEM(bwd.shape[1:], bf16),
            pltpu.VMEM(lon.shape, bf16),
            pltpu.VMEM(local.shape, bf16),
            pltpu.VMEM((layers, steps, channels, width), bf16),
            pltpu.VMEM((steps, width, width), bf16),
            pltpu.VMEM((modes * ROW_BLOCK, width), jnp.float32),
            pltpu.VMEM((ROW_BLOCK * channels, 2 * modes), bf16),
            pltpu.VMEM((many, many), bf16),
            dma((chunks,)), dma((5,)), dma((layers, steps)),
            dma((part_count,)), dma((slots,)), dma((2, steps)), dma((2, steps)),
            dma((part_count, group)), dma((part_count, group)),
            dma((steps, outer)), dma((steps, outer)),
            dma((steps, outer)), dma((steps, outer)),
            dma((slots, group)), dma((slots, group)),
        ],
        compiler_params=pltpu.CompilerParams(
            collective_id=0, has_side_effects=True, vmem_limit_bytes=NET_VMEM
        ),
        name="net_part",
    )(*operands)


def field_kernel(y_ref, local_ref, back_ref, out_ref, turned, turn, out_buf, out_sem):
    chunks, modes, rows, width = y_ref.shape
    channels = width // 2
    span = out_buf.shape[1]
    pieces = [(i, first) for i in range(chunks) for first in range(0, rows, span)]

    def out_copy(k):
        i, first = pieces[k]
        return pltpu.make_async_copy(
            out_buf.at[k % 2], out_ref.at[pl.ds(i * rows + first, span)], out_sem.at[k % 2]
        )

    for k, (i, first) in enumerate(pieces):
        if first == 0:
            spectrum_block(y_ref[i], turn, turned)
        if k >= 2:
            out_copy(k - 2).wait()
        own = slice(first * channels, (first + span) * channels)
        field_rows(
            0, span, local_ref.at[i, own], out_buf.at[k % 2], back_ref, turned.at[own]
        )
        out_copy(k).start()
    for k in range(max(0, len(pieces) - 2), len(pieces)):
        out_copy(k).wait()


def field_part(y, local, back):
    chunks, modes, rows, width = y.shape
    channels = width // 2
    lon_count = back.shape[1]
    span = max(1, min(rows, 256 // channels))
    vmem = pl.BlockSpec(memory_space=pltpu.VMEM)
    return pl.pallas_call(
        field_kernel,
        out_shape=jax.ShapeDtypeStruct((chunks * rows, channels, lon_count), jnp.bfloat16),
        in_specs=[vmem] * 3,
        out_specs=pl.BlockSpec(memory_space=pltpu.HBM),
        scratch_shapes=[
            pltpu.VMEM((rows * channels, 2 * modes), jnp.bfloat16),
            pltpu.VMEM((modes * rows, width), jnp.float32),
            pltpu.VMEM((2, span, channels, lon_count), jnp.bfloat16),
            pltpu.SemaphoreType.DMA((2,)),
        ],
        compiler_params=pltpu.CompilerParams(vmem_limit_bytes=FIELD_VMEM),
        name="field_part",
    )(y, local, back)


def shards(fields, spectral_weight, local_weight):
    row_count, channels, lon_count = fields.shape
    layer_count, mode_rows = spectral_weight.shape[:2]
    devices = lax.axis_size("lat")
    group = math.gcd(devices, 8)
    table = lon_table(lon_count, mode_rows)
    forward_lon = jnp.asarray(
        (table / math.sqrt(lon_count)).reshape(lon_count, 2 * mode_rows), jnp.bfloat16
    )
    backward_lon = jnp.asarray(
        (table.transpose(1, 2, 0) * (0.5 / math.sqrt(mode_rows))).reshape(
            2 * mode_rows, lon_count
        ),
        jnp.bfloat16,
    )
    forward_all, backward_all = lat_tables(devices, group, row_count, KY)
    forward_lat = jnp.asarray(forward_all, jnp.bfloat16)
    backward_lat = jnp.asarray(backward_all, jnp.bfloat16)
    y, local, back = net_part(
        fields, spectral_weight, forward_lat, backward_lat, forward_lon, backward_lon,
        local_weight, devices, group,
    )
    return field_part(y, local, back)


def solution(mesh):
    return jax.shard_map(
        shards,
        mesh=mesh,
        in_specs=(P(("grp", "lat"), None, None), P(), P()),
        out_specs=P(("grp", "lat"), None, None),
        check_vma=False,
    )
```

```python
import functools
import math

import jax
import jax.numpy as jnp
import numpy as np
from jax import lax
from jax.experimental import pallas as pl
from jax.experimental.pallas import tpu as pltpu
from jax.sharding import PartitionSpec as P

KY = 128
MESH = pl.DeviceIdType.MESH
LAG = (0, 1, 4, 5, 8)
ROW_BLOCK = 8
CHUNK = 512
NET_VMEM = 20 << 20
FIELD_VMEM = 8 << 20


def lon_table(lon_count, mode_count):
    cells = np.arange(lon_count, dtype=np.int64)[:, None]
    modes = np.arange(mode_count, dtype=np.int64)[None, :]
    angle = (2.0 * np.pi / lon_count) * (cells * modes % lon_count)
    return np.stack([np.cos(angle), -np.sin(angle)], axis=1)


def lat_tables(devices, group, row_count, kept):
    lat_count = devices * row_count
    outer = devices // group
    index = np.arange(kept, dtype=np.int64)
    waves = np.where(index < kept // 2, index, lat_count - kept + index)
    plane = np.arange(outer)[:, None, None, None]
    row = np.arange(row_count).reshape(1, -1, 1, ROW_BLOCK)
    inner = np.arange(group)[None, None, :, None]
    latitudes = (row * devices + plane * group + inner).reshape(outer, -1)
    angle = (2.0 * np.pi / lat_count) * (waves[None, :, None] * latitudes[:, None, :] % lat_count)
    both = np.concatenate([np.cos(angle), np.sin(angle)], axis=2) / math.sqrt(lat_count)
    turned = angle.transpose(0, 2, 1)
    back = np.concatenate([np.cos(turned), -np.sin(turned)], axis=2) / math.sqrt(kept)
    return both, back


def modes_out(flat, turn):
    width = turn.shape[1]
    channels = width // 2
    rows = flat.shape[0] // channels
    modes = flat.shape[1] // 2
    for n in range(rows):
        part = flat[n * channels:(n + 1) * channels]
        stacked = jnp.concatenate([part[:, :modes], part[:, modes:]], axis=0)
        turn[pl.ds(n, modes, stride=rows), :] = stacked.T
    return turn[...].reshape(modes, rows, width).astype(jnp.bfloat16)


def block_mixing(local, pointwise):
    channels = local.shape[0]
    pointwise[...] = jnp.zeros_like(pointwise)
    mixing = (local.astype(jnp.float32).T * 0.5).astype(jnp.bfloat16)
    for n in range(pointwise.shape[0] // channels):
        own = slice(n * channels, (n + 1) * channels)
        pointwise[own, own] = mixing


def pointwise_block(h_ref, out_ref, pointwise):
    rows, channels, lon_count = h_ref.shape
    many = pointwise.shape[0]
    span = many // channels
    chunk = min(CHUNK, lon_count)
    for first in range(0, rows, span):
        for column in range(0, lon_count, chunk):
            cells = slice(column, column + chunk)
            out_ref[first * channels:first * channels + many, cells] = jnp.dot(
                pointwise[...], h_ref[first:first + span, :, cells].reshape(many, chunk),
                preferred_element_type=jnp.float32,
            )


def spectrum_block(modes_in, turn, turned):
    modes, rows, width = modes_in.shape
    channels = width // 2
    turn[...] = modes_in.astype(jnp.float32).reshape(modes * rows, width)
    for n in range(rows):
        across = turn[pl.ds(n, modes, stride=rows), :].T
        turned[n * channels:(n + 1) * channels] = jnp.concatenate(
            [across[:channels], across[channels:]], axis=1
        ).astype(jnp.bfloat16)


def field_rows(first, span, local_ref, out_ref, back_ref, turned):
    _, channels, lon_count = out_ref.shape
    chunk = min(CHUNK, lon_count)
    inner = math.sqrt(2.0 / math.pi)
    own = slice(first * channels, (first + span) * channels)
    for column in range(0, lon_count, chunk):
        cells = slice(column, column + chunk)
        half = local_ref[own, cells] + jnp.dot(
            turned[own], back_ref[:, cells], preferred_element_type=jnp.float32
        )
        half = half.astype(jnp.bfloat16)
        curve = jnp.tanh(half * (2.0 * inner + (8.0 * inner * 0.044715) * (half * half)))
        out_ref[first:first + span, :, cells] = (
            (half * (1.0 + curve)).reshape(span, channels, chunk)
        )


def net_kernel(
    layers, group, outer, steps, order,
    h_ref, weight_ref, fwd_ref, bwd_ref, lon_ref, back_ref, mixing_ref, *rest,
):
    (
        y_ref, pw_buf, back_buf, h_buf, x_buf, r_buf, p_buf, q_buf, m_buf, v_buf, f_buf, acc,
        fwd_buf, bwd_buf, lon_buf, local_ref, w_buf, mix_buf, turn, turned, pointwise,
        h_sem, table_sem, w_sem, own_in_sem, own_out_sem, f_sem, g_sem,
        a_send, a_recv, b_send, b_recv, c_send, c_recv, d_send, d_recv,
    ) = rest
    span = pointwise.shape[0] // h_buf.shape[2]
    chunks, block, channels, lon_count = h_buf.shape
    modes, width = x_buf.shape[1], x_buf.shape[3]
    held = steps * outer
    kept = p_buf.shape[2]
    tall = chunks * group * block
    me = lax.axis_index("lat")
    z = me // group
    s = lax.rem(me, group)

    def inner_peer(i):
        return lax.rem(s + i, group)

    def outer_peer(i):
        return lax.rem(z + i, outer)

    def h_copy(i):
        return pltpu.make_async_copy(h_ref.at[pl.ds(i * block, block)], h_buf.at[i], h_sem.at[i])

    lon_copy = pltpu.make_async_copy(lon_ref, lon_buf, table_sem.at[0])
    local_copy = pltpu.make_async_copy(mixing_ref, local_ref, table_sem.at[4])
    back_copy = pltpu.make_async_copy(back_ref, back_buf, table_sem.at[1])
    fwd_copy = pltpu.make_async_copy(fwd_ref.at[z], fwd_buf, table_sem.at[2])
    bwd_copy = pltpu.make_async_copy(bwd_ref.at[z], bwd_buf, table_sem.at[3])
    w_copies = [
        pltpu.make_async_copy(
            weight_ref.at[l, (s * steps + t) * outer + z], w_buf.at[l, t], w_sem.at[l, t]
        )
        for l in range(layers) for t in range(steps)
    ]
    h_copy(0).start()
    lon_copy.start()
    for i in range(1, chunks):
        h_copy(i).start()

    barrier = pltpu.get_barrier_semaphore()
    for i in range(1, group):
        pl.semaphore_signal(
            barrier, inc=1, device_id={"lat": z * group + inner_peer(i)}, device_id_type=MESH
        )
    for i in range(1, outer):
        pl.semaphore_signal(
            barrier, inc=1, device_id={"lat": outer_peer(i) * group + s}, device_id_type=MESH
        )
    local_copy.start()
    fwd_copy.start()
    bwd_copy.start()
    for copy in w_copies:
        copy.start()
    back_copy.start()

    early = steps // 2

    def part_of(i, t):
        if t < early:
            return i * early + t, i, 1, t
        return chunks * early + t - early, 0, chunks, t

    def parts_of(t):
        return [part_of(i, t) for i in range(chunks if t < early else 1)]

    def a_copy(part, i):
        to = inner_peer(i)
        slot, c0, nc, t = part
        return pltpu.make_async_remote_copy(
            src_ref=x_buf.at[pl.ds(c0, nc), pl.ds(to * held + t * outer, outer)],
            dst_ref=r_buf.at[pl.ds(c0, nc), s, pl.ds(t * outer, outer)],
            send_sem=a_send.at[slot, i], recv_sem=a_recv.at[slot, i],
            device_id={"lat": z * group + to}, device_id_type=MESH,
        )

    def own_in(part):
        slot, c0, nc, t = part
        return pltpu.make_async_copy(
            x_buf.at[pl.ds(c0, nc), pl.ds(s * held + t * outer, outer)],
            r_buf.at[pl.ds(c0, nc), s, pl.ds(t * outer, outer)],
            own_in_sem.at[slot],
        )

    def b_copy(t, i):
        to = outer_peer(i)
        return pltpu.make_async_remote_copy(
            src_ref=p_buf.at[t, to], dst_ref=q_buf.at[t, z],
            send_sem=b_send.at[t, i], recv_sem=b_recv.at[t, i],
            device_id={"lat": to * group + s}, device_id_type=MESH,
        )

    def c_copy(t, i):
        to = outer_peer(i)
        return pltpu.make_async_remote_copy(
            src_ref=m_buf.at[t, z], dst_ref=m_buf.at[t, z],
            send_sem=c_send.at[t, i], recv_sem=c_recv.at[t, i],
            device_id={"lat": to * group + s}, device_id_type=MESH,
        )

    def d_copy(slot, c0, nc, t, i):
        to = inner_peer(i)
        return pltpu.make_async_remote_copy(
            src_ref=v_buf.at[pl.ds(c0, nc), to, pl.ds(t * outer, outer)],
            dst_ref=y_ref.at[pl.ds(c0, nc), pl.ds((s * steps + t) * outer, outer)],
            send_sem=d_send.at[slot, i], recv_sem=d_recv.at[slot, i],
            device_id={"lat": z * group + to}, device_id_type=MESH,
        )

    def own_out(slot, c0, nc, t):
        return pltpu.make_async_copy(
            v_buf.at[pl.ds(c0, nc), s, pl.ds(t * outer, outer)],
            y_ref.at[pl.ds(c0, nc), pl.ds((s * steps + t) * outer, outer)],
            own_out_sem.at[slot],
        )

    d_parts = [(t, 0, chunks, t) for t in range(steps - 1)]
    d_parts += [(steps - 1 + c, c, 1, steps - 1) for c in range(chunks)]

    def f_copy(t):
        return pltpu.make_async_remote_copy(
            src_ref=p_buf.at[t, outer - 1 - z], dst_ref=f_buf.at[t],
            send_sem=f_sem.at[0, t], recv_sem=f_sem.at[1, t],
            device_id={"lat": jnp.where(z == 0, 1, outer - 2) * group + s}, device_id_type=MESH,
        )

    def g_copy(t):
        block_of = outer_peer(2)
        return pltpu.make_async_remote_copy(
            src_ref=m_buf.at[t, block_of], dst_ref=m_buf.at[t, block_of],
            send_sem=g_sem.at[0, t], recv_sem=g_sem.at[1, t],
            device_id={"lat": (outer - 1 - block_of) * group + s}, device_id_type=MESH,
        )

    relay = outer == 4
    last = outer - 1
    at_end = jnp.logical_or(z == 0, z == last)
    inside = jnp.logical_not(at_end)
    lane = lax.broadcasted_iota(jnp.int32, (1, width), 1)
    sign = jnp.where(lane < channels, 1.0, -1.0)

    def swapped(values):
        return (pltpu.roll(values.astype(jnp.float32), channels, 1) * sign).astype(jnp.bfloat16)

    def lon_block(i):
        flat = jnp.dot(
            h_buf[i].reshape(block * channels, lon_count), lon_buf[...],
            preferred_element_type=jnp.float32,
        )
        x_buf[i] = modes_out(flat, turn)

    def send_part(part):
        own_in(part).start()
        for i in range(1, group):
            a_copy(part, i).start()

    def send_head(i):
        for t in range(early):
            send_part(part_of(i, t))

    def send_tail():
        for t in range(early, steps):
            send_part(part_of(0, t))

    def forward(t):
        for part in parts_of(t):
            own_in(part).wait()
            for i in range(1, group):
                a_copy(part, i).wait_recv()
        for first in range(0, outer, 2):
            pair = []
            for u in range(first, min(first + 2, outer)):
                values = r_buf[:, :, t * outer + u].reshape(tall, width)
                pair.append(jnp.concatenate([values, swapped(values)], axis=0))
            out = jnp.dot(
                fwd_buf[...], jnp.concatenate(pair, axis=1), preferred_element_type=jnp.float32
            ).astype(jnp.bfloat16)
            for u in range(len(pair)):
                p_buf[t, first + u] = out[:, u * width:(u + 1) * width]
        if not relay:
            for i in range(1, outer):
                b_copy(t, i).start()
            return
        pl.when(at_end)(lambda: f_copy(t).start())
        pl.when(at_end)(lambda: b_copy(t, 2).start())
        pl.when(z != last)(lambda: b_copy(t, 1).start())
        pl.when(z != 0)(lambda: b_copy(t, last).start())

    def relay_sum(t):
        if not relay:
            return

        @pl.when(inside)
        def _():
            f_copy(t).wait_recv()
            to = outer_peer(2)
            p_buf[t, to] = (
                p_buf[t, to].astype(jnp.float32) + f_buf[t].astype(jnp.float32)
            ).astype(jnp.bfloat16)
            b_copy(t, 2).start()

    def collect(t, i):
        b_copy(t, i).wait_recv()
        acc[...] += q_buf[t, lax.rem(z + outer - i, outer)].astype(jnp.float32)

    def middle(t):
        acc[...] = p_buf[t, z].astype(jnp.float32)
        if relay:
            pl.when(z != 0)(lambda: collect(t, 1))
            pl.when(z != last)(lambda: collect(t, last))
            collect(t, 2)
        else:
            for i in range(1, outer):
                collect(t, i)
        mixed = jnp.dot(
            acc[...].astype(jnp.bfloat16), mix_buf[t], preferred_element_type=jnp.float32
        )
        m_buf[t, z] = mixed.astype(jnp.bfloat16)
        if relay:
            c_copy(t, 2).start()
            pl.when(z != last)(lambda: c_copy(t, 1).start())
            pl.when(z != 0)(lambda: c_copy(t, last).start())
        else:
            for i in range(1, outer):
                c_copy(t, i).start()

    def relay_out(t):
        if not relay:
            return

        @pl.when(inside)
        def _():
            c_copy(t, 2).wait_recv()
            g_copy(t).start()

    def backward(t):
        if relay:
            pl.when(z != 0)(lambda: c_copy(t, 1).wait_recv())
            pl.when(z != last)(lambda: c_copy(t, last).wait_recv())
            pl.when(at_end)(lambda: c_copy(t, 2).wait_recv())
            pl.when(at_end)(lambda: g_copy(t).wait_recv())
        else:
            for i in range(1, outer):
                c_copy(t, i).wait_recv()
        for first in range(0, outer, 2):
            pair = []
            for u in range(first, min(first + 2, outer)):
                values = m_buf[t, u]
                pair.append(jnp.concatenate([values, swapped(values)], axis=0))
            out = jnp.dot(
                bwd_buf[...], jnp.concatenate(pair, axis=1), preferred_element_type=jnp.float32
            ).astype(jnp.bfloat16)
            for u in range(len(pair)):
                v_buf[:, :, t * outer + first + u] = out[:, u * width:(u + 1) * width].reshape(
                    chunks, group, block, width
                )
        for slot, c0, nc, _ in [p for p in d_parts if p[3] == t]:
            for i in range(1, group):
                d_copy(slot, c0, nc, t, i).start()
            own_out(slot, c0, nc, t).start()

    def landed(slot, c0, nc, t):
        own_out(slot, c0, nc, t).wait()
        for i in range(1, group):
            d_copy(slot, c0, nc, t, i).wait_recv()

    def lat_sent():
        for t in range(steps):
            for part in parts_of(t):
                for i in range(1, group):
                    a_copy(part, i).wait_send()
        for t in range(steps):
            if relay:
                pl.when(at_end)(lambda: f_copy(t).wait_send())
                pl.when(inside)(lambda: g_copy(t).wait_send())
                for copy in (b_copy, c_copy):
                    copy(t, 2).wait_send()
                    pl.when(z != last)(lambda: copy(t, 1).wait_send())
                    pl.when(z != 0)(lambda: copy(t, last).wait_send())
            else:
                for i in range(1, outer):
                    b_copy(t, i).wait_send()
                    c_copy(t, i).wait_send()

    def back_sent():
        for slot, c0, nc, t in d_parts:
            for i in range(1, group):
                d_copy(slot, c0, nc, t, i).wait_send()

    stages = {
        "forward": forward, "relay_sum": relay_sum, "middle": middle,
        "relay_out": relay_out, "backward": backward,
    }

    def lat_block(layer):
        for t in range(steps):
            weight = w_buf[layer, t].astype(jnp.float32)
            mix_buf[t, :channels] = w_buf[layer, t]
            mix_buf[t, channels:] = (
                pltpu.roll(weight, channels, 1) * -sign
            ).astype(jnp.bfloat16)
        block_mixing(local_ref[layer], pointwise)

        @pl.loop(0, chunks)
        def _(i):
            pointwise_block(h_buf.at[i], pw_buf.at[i], pointwise)

        for name, t in order:
            stages[name](t)
        for part in d_parts[:steps - 1]:
            landed(*part)
        lat_sent()

    lon_copy.wait()

    @pl.loop(0, chunks)
    def _(i):
        h_copy(i).wait()
        lon_block(i)
        pl.when(i == 0)(lambda: pl.semaphore_wait(barrier, group - 1 + outer - 1))
        send_head(i)

    send_tail()
    local_copy.wait()
    fwd_copy.wait()
    bwd_copy.wait()
    for copy in w_copies:
        copy.wait()
    back_copy.wait()

    @pl.loop(0, layers)
    def _(layer):
        lat_block(layer)

        @pl.when(layer < layers - 1)
        def _():
            @pl.loop(0, chunks)
            def _(i):
                landed(steps - 1 + i, i, 1, steps - 1)
                spectrum_block(y_ref[i], turn, turned)
                for first in range(0, block, span):
                    field_rows(first, span, pw_buf.at[i], h_buf.at[i], back_buf, turned)
                lon_block(i)
                send_head(i)

        @pl.when(layer == layers - 1)
        def _():
            for part in d_parts[steps - 1:]:
                landed(*part)
        back_sent()
        pl.when(layer < layers - 1)(send_tail)


def schedule(steps, lags):
    names = ("forward", "relay_sum", "middle", "relay_out", "backward")
    return [
        (name, step - lag)
        for step in range(steps + max(lags))
        for name, lag in zip(names, lags)
        if 0 <= step - lag < steps
    ]


def net_part(h, weight, fwd, bwd, lon, back, local, devices, group):
    rows, channels, lon_count = h.shape
    layers, modes, _, width = weight.shape
    outer = devices // group
    steps = modes // devices
    chunks = rows // ROW_BLOCK
    kept = fwd.shape[1]
    held = steps * outer
    dma = pltpu.SemaphoreType.DMA
    vmem = pl.BlockSpec(memory_space=pltpu.VMEM)
    hbm = pl.BlockSpec(memory_space=pltpu.HBM)
    bf16 = jnp.bfloat16
    many = max(1, min(ROW_BLOCK, 256 // channels)) * channels
    shapes = [
        jax.ShapeDtypeStruct((chunks, modes, ROW_BLOCK, width), bf16),
        jax.ShapeDtypeStruct((chunks, ROW_BLOCK * channels, lon_count), jnp.float32),
        jax.ShapeDtypeStruct(back.shape, bf16),
    ]
    part_count = chunks * (steps // 2) + steps - steps // 2
    slots = steps - 1 + chunks
    operands = [
        pltpu.with_memory_space_constraint(a, pltpu.HBM)
        for a in (h, weight, fwd, bwd, lon, back, local)
    ]
    return pl.pallas_call(
        functools.partial(net_kernel, layers, group, outer, steps, schedule(steps, LAG)),
        out_shape=shapes,
        in_specs=[hbm] * 7,
        out_specs=[vmem] * 3,
        scratch_shapes=[
            pltpu.VMEM((chunks, ROW_BLOCK, channels, lon_count), bf16),
            pltpu.VMEM((chunks, modes, ROW_BLOCK, width), bf16),
            pltpu.VMEM((chunks, group, held, ROW_BLOCK, width), bf16),
            pltpu.VMEM((steps, outer, kept, width), bf16),
            pltpu.VMEM((steps, outer, kept, width), bf16),
            pltpu.VMEM((steps, outer, kept, width), bf16),
            pltpu.VMEM((chunks, group, held, ROW_BLOCK, width), bf16),
            pltpu.VMEM((steps, kept, width), bf16),
            pltpu.VMEM((kept, width), jnp.float32),
            pltpu.VMEM(fwd.shape[1:], bf16),
            pltpu.VMEM(bwd.shape[1:], bf16),
            pltpu.VMEM(lon.shape, bf16),
            pltpu.VMEM(local.shape, bf16),
            pltpu.VMEM((layers, steps, channels, width), bf16),
            pltpu.VMEM((steps, width, width), bf16),
            pltpu.VMEM((modes * ROW_BLOCK, width), jnp.float32),
            pltpu.VMEM((ROW_BLOCK * channels, 2 * modes), bf16),
            pltpu.VMEM((many, many), bf16),
            dma((chunks,)), dma((5,)), dma((layers, steps)),
            dma((part_count,)), dma((slots,)), dma((2, steps)), dma((2, steps)),
            dma((part_count, group)), dma((part_count, group)),
            dma((steps, outer)), dma((steps, outer)),
            dma((steps, outer)), dma((steps, outer)),
            dma((slots, group)), dma((slots, group)),
        ],
        compiler_params=pltpu.CompilerParams(
            collective_id=0, has_side_effects=True, vmem_limit_bytes=NET_VMEM
        ),
        name="net_part",
    )(*operands)


def field_kernel(y_ref, local_ref, back_ref, out_ref, turned, turn, out_buf, out_sem):
    chunks, modes, rows, width = y_ref.shape
    channels = width // 2
    span = out_buf.shape[1]
    pieces = [(i, first) for i in range(chunks) for first in range(0, rows, span)]

    def out_copy(k):
        i, first = pieces[k]
        return pltpu.make_async_copy(
            out_buf.at[k % 2], out_ref.at[pl.ds(i * rows + first, span)], out_sem.at[k % 2]
        )

    for k, (i, first) in enumerate(pieces):
        if first == 0:
            spectrum_block(y_ref[i], turn, turned)
        if k >= 2:
            out_copy(k - 2).wait()
        own = slice(first * channels, (first + span) * channels)
        field_rows(
            0, span, local_ref.at[i, own], out_buf.at[k % 2], back_ref, turned.at[own]
        )
        out_copy(k).start()
    for k in range(max(0, len(pieces) - 2), len(pieces)):
        out_copy(k).wait()


def field_part(y, local, back):
    chunks, modes, rows, width = y.shape
    channels = width // 2
    lon_count = back.shape[1]
    span = max(1, min(rows, 256 // channels))
    vmem = pl.BlockSpec(memory_space=pltpu.VMEM)
    return pl.pallas_call(
        field_kernel,
        out_shape=jax.ShapeDtypeStruct((chunks * rows, channels, lon_count), jnp.bfloat16),
        in_specs=[vmem] * 3,
        out_specs=pl.BlockSpec(memory_space=pltpu.HBM),
        scratch_shapes=[
            pltpu.VMEM((rows * channels, 2 * modes), jnp.bfloat16),
            pltpu.VMEM((modes * rows, width), jnp.float32),
            pltpu.VMEM((2, span, channels, lon_count), jnp.bfloat16),
            pltpu.SemaphoreType.DMA((2,)),
        ],
        compiler_params=pltpu.CompilerParams(vmem_limit_bytes=FIELD_VMEM),
        name="field_part",
    )(y, local, back)


def shards(fields, spectral_weight, local_weight):
    row_count, channels, lon_count = fields.shape
    layer_count, mode_rows = spectral_weight.shape[:2]
    devices = lax.axis_size("lat")
    group = math.gcd(devices, 16)
    table = lon_table(lon_count, mode_rows)
    forward_lon = jnp.asarray(
        (table / math.sqrt(lon_count)).reshape(lon_count, 2 * mode_rows), jnp.bfloat16
    )
    backward_lon = jnp.asarray(
        (table.transpose(1, 2, 0) * (0.5 / math.sqrt(mode_rows))).reshape(
            2 * mode_rows, lon_count
        ),
        jnp.bfloat16,
    )
    forward_all, backward_all = lat_tables(devices, group, row_count, KY)
    forward_lat = jnp.asarray(forward_all, jnp.bfloat16)
    backward_lat = jnp.asarray(backward_all, jnp.bfloat16)
    y, local, back = net_part(
        fields, spectral_weight, forward_lat, backward_lat, forward_lon, backward_lon,
        local_weight, devices, group,
    )
    return field_part(y, local, back)


def solution(mesh):
    return jax.shard_map(
        shards,
        mesh=mesh,
        in_specs=(P(("grp", "lat"), None, None), P(), P()),
        out_specs=P(("grp", "lat"), None, None),
        check_vma=False,
    )
```

```python
import functools
import math

import jax
import jax.numpy as jnp
import numpy as np
from jax import lax
from jax.experimental import pallas as pl
from jax.experimental.pallas import tpu as pltpu
from jax.sharding import PartitionSpec as P

KY = 128
MESH = pl.DeviceIdType.MESH
LAG = (0, 1, 2, 3, 4)
ROW_BLOCK = 8
CHUNK = 512
NET_VMEM = 20 << 20
FIELD_VMEM = 8 << 20


def lon_table(lon_count, mode_count):
    cells = np.arange(lon_count, dtype=np.int64)[:, None]
    modes = np.arange(mode_count, dtype=np.int64)[None, :]
    angle = (2.0 * np.pi / lon_count) * (cells * modes % lon_count)
    return np.stack([np.cos(angle), -np.sin(angle)], axis=1)


def lat_tables(devices, group, row_count, kept):
    lat_count = devices * row_count
    outer = devices // group
    index = np.arange(kept, dtype=np.int64)
    waves = np.where(index < kept // 2, index, lat_count - kept + index)
    plane = np.arange(outer)[:, None, None, None]
    row = np.arange(row_count).reshape(1, -1, 1, ROW_BLOCK)
    inner = np.arange(group)[None, None, :, None]
    latitudes = (row * devices + plane * group + inner).reshape(outer, -1)
    angle = (2.0 * np.pi / lat_count) * (waves[None, :, None] * latitudes[:, None, :] % lat_count)
    both = np.concatenate([np.cos(angle), np.sin(angle)], axis=2) / math.sqrt(lat_count)
    turned = angle.transpose(0, 2, 1)
    back = np.concatenate([np.cos(turned), -np.sin(turned)], axis=2) / math.sqrt(kept)
    return both, back


def modes_out(flat, turn):
    width = turn.shape[1]
    channels = width // 2
    rows = flat.shape[0] // channels
    modes = flat.shape[1] // 2
    for n in range(rows):
        part = flat[n * channels:(n + 1) * channels]
        stacked = jnp.concatenate([part[:, :modes], part[:, modes:]], axis=0)
        turn[pl.ds(n, modes, stride=rows), :] = stacked.T
    return turn[...].reshape(modes, rows, width).astype(jnp.bfloat16)


def block_mixing(local, pointwise):
    channels = local.shape[0]
    pointwise[...] = jnp.zeros_like(pointwise)
    mixing = (local.astype(jnp.float32).T * 0.5).astype(jnp.bfloat16)
    for n in range(pointwise.shape[0] // channels):
        own = slice(n * channels, (n + 1) * channels)
        pointwise[own, own] = mixing


def pointwise_block(h_ref, out_ref, pointwise):
    rows, channels, lon_count = h_ref.shape
    many = pointwise.shape[0]
    span = many // channels
    chunk = min(CHUNK, lon_count)
    for first in range(0, rows, span):
        for column in range(0, lon_count, chunk):
            cells = slice(column, column + chunk)
            out_ref[first * channels:first * channels + many, cells] = jnp.dot(
                pointwise[...], h_ref[first:first + span, :, cells].reshape(many, chunk),
                preferred_element_type=jnp.float32,
            )


def spectrum_block(modes_in, turn, turned):
    modes, rows, width = modes_in.shape
    channels = width // 2
    turn[...] = modes_in.astype(jnp.float32).reshape(modes * rows, width)
    for n in range(rows):
        across = turn[pl.ds(n, modes, stride=rows), :].T
        turned[n * channels:(n + 1) * channels] = jnp.concatenate(
            [across[:channels], across[channels:]], axis=1
        ).astype(jnp.bfloat16)


def field_rows(first, span, local_ref, out_ref, back_ref, turned):
    _, channels, lon_count = out_ref.shape
    chunk = min(CHUNK, lon_count)
    inner = math.sqrt(2.0 / math.pi)
    own = slice(first * channels, (first + span) * channels)
    for column in range(0, lon_count, chunk):
        cells = slice(column, column + chunk)
        half = local_ref[own, cells] + jnp.dot(
            turned[own], back_ref[:, cells], preferred_element_type=jnp.float32
        )
        half = half.astype(jnp.bfloat16)
        curve = jnp.tanh(half * (2.0 * inner + (8.0 * inner * 0.044715) * (half * half)))
        out_ref[first:first + span, :, cells] = (
            (half * (1.0 + curve)).reshape(span, channels, chunk)
        )


def net_kernel(
    layers, group, outer, steps, order,
    h_ref, weight_ref, fwd_ref, bwd_ref, lon_ref, back_ref, mixing_ref, *rest,
):
    (
        y_ref, pw_buf, back_buf, h_buf, x_buf, r_buf, p_buf, q_buf, m_buf, v_buf, f_buf, acc,
        fwd_buf, bwd_buf, lon_buf, local_ref, w_buf, mix_buf, turn, turned, pointwise,
        h_sem, table_sem, w_sem, own_in_sem, own_out_sem, f_sem, g_sem,
        a_send, a_recv, b_send, b_recv, c_send, c_recv, d_send, d_recv,
    ) = rest
    span = pointwise.shape[0] // h_buf.shape[2]
    chunks, block, channels, lon_count = h_buf.shape
    modes, width = x_buf.shape[1], x_buf.shape[3]
    held = steps * outer
    kept = p_buf.shape[2]
    tall = chunks * group * block
    me = lax.axis_index("lat")
    z = me // group
    s = lax.rem(me, group)

    def inner_peer(i):
        return lax.rem(s + i, group)

    def outer_peer(i):
        return lax.rem(z + i, outer)

    def h_copy(i):
        return pltpu.make_async_copy(h_ref.at[pl.ds(i * block, block)], h_buf.at[i], h_sem.at[i])

    lon_copy = pltpu.make_async_copy(lon_ref, lon_buf, table_sem.at[0])
    local_copy = pltpu.make_async_copy(mixing_ref, local_ref, table_sem.at[4])
    back_copy = pltpu.make_async_copy(back_ref, back_buf, table_sem.at[1])
    fwd_copy = pltpu.make_async_copy(fwd_ref.at[z], fwd_buf, table_sem.at[2])
    bwd_copy = pltpu.make_async_copy(bwd_ref.at[z], bwd_buf, table_sem.at[3])
    w_copies = [
        pltpu.make_async_copy(
            weight_ref.at[l, (s * steps + t) * outer + z], w_buf.at[l, t], w_sem.at[l, t]
        )
        for l in range(layers) for t in range(steps)
    ]
    h_copy(0).start()
    lon_copy.start()
    for i in range(1, chunks):
        h_copy(i).start()

    barrier = pltpu.get_barrier_semaphore()
    for i in range(1, group):
        pl.semaphore_signal(
            barrier, inc=1, device_id={"lat": z * group + inner_peer(i)}, device_id_type=MESH
        )
    for i in range(1, outer):
        pl.semaphore_signal(
            barrier, inc=1, device_id={"lat": outer_peer(i) * group + s}, device_id_type=MESH
        )
    local_copy.start()
    fwd_copy.start()
    bwd_copy.start()
    for copy in w_copies:
        copy.start()
    back_copy.start()

    early = steps // 2

    def early_part(i):
        return i, i, 1, 0, early * outer

    def late_part(t):
        return chunks + t - early, 0, chunks, t * outer, outer

    def parts_of(t):
        if t >= early:
            return [late_part(t)]
        return [early_part(i) for i in range(chunks)] if t == 0 else []

    def a_copy(part, i):
        to = inner_peer(i)
        slot, c0, nc, m0, nm = part
        return pltpu.make_async_remote_copy(
            src_ref=x_buf.at[pl.ds(c0, nc), pl.ds(to * held + m0, nm)],
            dst_ref=r_buf.at[pl.ds(c0, nc), s, pl.ds(m0, nm)],
            send_sem=a_send.at[slot, i], recv_sem=a_recv.at[slot, i],
            device_id={"lat": z * group + to}, device_id_type=MESH,
        )

    def own_in(part):
        slot, c0, nc, m0, nm = part
        return pltpu.make_async_copy(
            x_buf.at[pl.ds(c0, nc), pl.ds(s * held + m0, nm)],
            r_buf.at[pl.ds(c0, nc), s, pl.ds(m0, nm)],
            own_in_sem.at[slot],
        )

    def b_copy(t, i):
        to = outer_peer(i)
        return pltpu.make_async_remote_copy(
            src_ref=p_buf.at[t, to], dst_ref=q_buf.at[t, z],
            send_sem=b_send.at[t, i], recv_sem=b_recv.at[t, i],
            device_id={"lat": to * group + s}, device_id_type=MESH,
        )

    def c_copy(t, i):
        to = outer_peer(i)
        return pltpu.make_async_remote_copy(
            src_ref=m_buf.at[t, z], dst_ref=m_buf.at[t, z],
            send_sem=c_send.at[t, i], recv_sem=c_recv.at[t, i],
            device_id={"lat": to * group + s}, device_id_type=MESH,
        )

    def d_copy(slot, c0, nc, t, i):
        to = inner_peer(i)
        return pltpu.make_async_remote_copy(
            src_ref=v_buf.at[pl.ds(c0, nc), to, pl.ds(t * outer, outer)],
            dst_ref=y_ref.at[pl.ds(c0, nc), pl.ds((s * steps + t) * outer, outer)],
            send_sem=d_send.at[slot, i], recv_sem=d_recv.at[slot, i],
            device_id={"lat": z * group + to}, device_id_type=MESH,
        )

    def own_out(slot, c0, nc, t):
        return pltpu.make_async_copy(
            v_buf.at[pl.ds(c0, nc), s, pl.ds(t * outer, outer)],
            y_ref.at[pl.ds(c0, nc), pl.ds((s * steps + t) * outer, outer)],
            own_out_sem.at[slot],
        )

    d_parts = [(t, 0, chunks, t) for t in range(steps)]

    def f_copy(t):
        return pltpu.make_async_remote_copy(
            src_ref=p_buf.at[t, outer - 1 - z], dst_ref=f_buf.at[t],
            send_sem=f_sem.at[0, t], recv_sem=f_sem.at[1, t],
            device_id={"lat": jnp.where(z == 0, 1, outer - 2) * group + s}, device_id_type=MESH,
        )

    def g_copy(t):
        block_of = outer_peer(2)
        return pltpu.make_async_remote_copy(
            src_ref=m_buf.at[t, block_of], dst_ref=m_buf.at[t, block_of],
            send_sem=g_sem.at[0, t], recv_sem=g_sem.at[1, t],
            device_id={"lat": (outer - 1 - block_of) * group + s}, device_id_type=MESH,
        )

    relay = outer == 4
    last = outer - 1
    at_end = jnp.logical_or(z == 0, z == last)
    inside = jnp.logical_not(at_end)
    lane = lax.broadcasted_iota(jnp.int32, (1, width), 1)
    sign = jnp.where(lane < channels, 1.0, -1.0)

    def swapped(values):
        return (pltpu.roll(values.astype(jnp.float32), channels, 1) * sign).astype(jnp.bfloat16)

    def lon_block(i):
        flat = jnp.dot(
            h_buf[i].reshape(block * channels, lon_count), lon_buf[...],
            preferred_element_type=jnp.float32,
        )
        x_buf[i] = modes_out(flat, turn)

    def send_part(part):
        own_in(part).start()
        for i in range(1, group):
            a_copy(part, i).start()

    def send_head(i):
        if early:
            send_part(early_part(i))

    def send_tail():
        for t in range(early, steps):
            send_part(late_part(t))

    def forward(t):
        for part in parts_of(t):
            own_in(part).wait()
            for i in range(1, group):
                a_copy(part, i).wait_recv()
        for first in range(0, outer, 2):
            pair = []
            for u in range(first, min(first + 2, outer)):
                values = r_buf[:, :, t * outer + u].reshape(tall, width)
                pair.append(jnp.concatenate([values, swapped(values)], axis=0))
            out = jnp.dot(
                fwd_buf[...], jnp.concatenate(pair, axis=1), preferred_element_type=jnp.float32
            ).astype(jnp.bfloat16)
            for u in range(len(pair)):
                p_buf[t, first + u] = out[:, u * width:(u + 1) * width]
        if not relay:
            for i in range(1, outer):
                b_copy(t, i).start()
            return
        pl.when(at_end)(lambda: f_copy(t).start())
        pl.when(at_end)(lambda: b_copy(t, 2).start())
        pl.when(z != last)(lambda: b_copy(t, 1).start())
        pl.when(z != 0)(lambda: b_copy(t, last).start())

    def relay_sum(t):
        if not relay:
            return

        @pl.when(inside)
        def _():
            f_copy(t).wait_recv()
            to = outer_peer(2)
            p_buf[t, to] = (
                p_buf[t, to].astype(jnp.float32) + f_buf[t].astype(jnp.float32)
            ).astype(jnp.bfloat16)
            b_copy(t, 2).start()

    def collect(t, i):
        b_copy(t, i).wait_recv()
        acc[...] += q_buf[t, lax.rem(z + outer - i, outer)].astype(jnp.float32)

    def middle(t):
        acc[...] = p_buf[t, z].astype(jnp.float32)
        if relay:
            pl.when(z != 0)(lambda: collect(t, 1))
            pl.when(z != last)(lambda: collect(t, last))
            collect(t, 2)
        else:
            for i in range(1, outer):
                collect(t, i)
        mixed = jnp.dot(
            acc[...].astype(jnp.bfloat16), mix_buf[t], preferred_element_type=jnp.float32
        )
        m_buf[t, z] = mixed.astype(jnp.bfloat16)
        if relay:
            c_copy(t, 2).start()
            pl.when(z != last)(lambda: c_copy(t, 1).start())
            pl.when(z != 0)(lambda: c_copy(t, last).start())
        else:
            for i in range(1, outer):
                c_copy(t, i).start()

    def relay_out(t):
        if not relay:
            return

        @pl.when(inside)
        def _():
            c_copy(t, 2).wait_recv()
            g_copy(t).start()

    def backward(t):
        if relay:
            pl.when(z != 0)(lambda: c_copy(t, 1).wait_recv())
            pl.when(z != last)(lambda: c_copy(t, last).wait_recv())
            pl.when(at_end)(lambda: c_copy(t, 2).wait_recv())
            pl.when(at_end)(lambda: g_copy(t).wait_recv())
        else:
            for i in range(1, outer):
                c_copy(t, i).wait_recv()
        for first in range(0, outer, 2):
            pair = []
            for u in range(first, min(first + 2, outer)):
                values = m_buf[t, u]
                pair.append(jnp.concatenate([values, swapped(values)], axis=0))
            out = jnp.dot(
                bwd_buf[...], jnp.concatenate(pair, axis=1), preferred_element_type=jnp.float32
            ).astype(jnp.bfloat16)
            for u in range(len(pair)):
                v_buf[:, :, t * outer + first + u] = out[:, u * width:(u + 1) * width].reshape(
                    chunks, group, block, width
                )
        for slot, c0, nc, _ in [p for p in d_parts if p[3] == t]:
            for i in range(1, group):
                d_copy(slot, c0, nc, t, i).start()
            own_out(slot, c0, nc, t).start()

    def landed(slot, c0, nc, t):
        own_out(slot, c0, nc, t).wait()
        for i in range(1, group):
            d_copy(slot, c0, nc, t, i).wait_recv()

    def lat_sent():
        for t in range(steps):
            for part in parts_of(t):
                for i in range(1, group):
                    a_copy(part, i).wait_send()
        for t in range(steps):
            if relay:
                pl.when(at_end)(lambda: f_copy(t).wait_send())
                pl.when(inside)(lambda: g_copy(t).wait_send())
                for copy in (b_copy, c_copy):
                    copy(t, 2).wait_send()
                    pl.when(z != last)(lambda: copy(t, 1).wait_send())
                    pl.when(z != 0)(lambda: copy(t, last).wait_send())
            else:
                for i in range(1, outer):
                    b_copy(t, i).wait_send()
                    c_copy(t, i).wait_send()

    def back_sent():
        for slot, c0, nc, t in d_parts:
            for i in range(1, group):
                d_copy(slot, c0, nc, t, i).wait_send()

    stages = {
        "forward": forward, "relay_sum": relay_sum, "middle": middle,
        "relay_out": relay_out, "backward": backward,
    }

    def lat_block(layer):
        for t in range(steps):
            weight = w_buf[layer, t].astype(jnp.float32)
            mix_buf[t, :channels] = w_buf[layer, t]
            mix_buf[t, channels:] = (
                pltpu.roll(weight, channels, 1) * -sign
            ).astype(jnp.bfloat16)
        block_mixing(local_ref[layer], pointwise)

        @pl.loop(0, chunks)
        def _(i):
            pointwise_block(h_buf.at[i], pw_buf.at[i], pointwise)

        for name, t in order:
            stages[name](t)
        for part in d_parts:
            landed(*part)
        lat_sent()

    lon_copy.wait()

    @pl.loop(0, chunks)
    def _(i):
        h_copy(i).wait()
        lon_block(i)
        pl.when(i == 0)(lambda: pl.semaphore_wait(barrier, group - 1 + outer - 1))
        send_head(i)

    send_tail()
    local_copy.wait()
    fwd_copy.wait()
    bwd_copy.wait()
    for copy in w_copies:
        copy.wait()
    back_copy.wait()

    @pl.loop(0, layers)
    def _(layer):
        lat_block(layer)

        @pl.when(layer < layers - 1)
        def _():
            @pl.loop(0, chunks)
            def _(i):
                spectrum_block(y_ref[i], turn, turned)
                for first in range(0, block, span):
                    field_rows(first, span, pw_buf.at[i], h_buf.at[i], back_buf, turned)
                lon_block(i)
                send_head(i)

        back_sent()
        pl.when(layer < layers - 1)(send_tail)


def schedule(steps, lags):
    names = ("forward", "relay_sum", "middle", "relay_out", "backward")
    return [
        (name, step - lag)
        for step in range(steps + max(lags))
        for name, lag in zip(names, lags)
        if 0 <= step - lag < steps
    ]


def net_part(h, weight, fwd, bwd, lon, back, local, devices, group):
    rows, channels, lon_count = h.shape
    layers, modes, _, width = weight.shape
    outer = devices // group
    steps = modes // devices
    chunks = rows // ROW_BLOCK
    kept = fwd.shape[1]
    held = steps * outer
    dma = pltpu.SemaphoreType.DMA
    vmem = pl.BlockSpec(memory_space=pltpu.VMEM)
    hbm = pl.BlockSpec(memory_space=pltpu.HBM)
    bf16 = jnp.bfloat16
    many = max(1, min(ROW_BLOCK, 256 // channels)) * channels
    shapes = [
        jax.ShapeDtypeStruct((chunks, modes, ROW_BLOCK, width), bf16),
        jax.ShapeDtypeStruct((chunks, ROW_BLOCK * channels, lon_count), jnp.float32),
        jax.ShapeDtypeStruct(back.shape, bf16),
    ]
    part_count = chunks + steps - steps // 2
    slots = steps
    operands = [
        pltpu.with_memory_space_constraint(a, pltpu.HBM)
        for a in (h, weight, fwd, bwd, lon, back, local)
    ]
    return pl.pallas_call(
        functools.partial(net_kernel, layers, group, outer, steps, schedule(steps, LAG)),
        out_shape=shapes,
        in_specs=[hbm] * 7,
        out_specs=[vmem] * 3,
        scratch_shapes=[
            pltpu.VMEM((chunks, ROW_BLOCK, channels, lon_count), bf16),
            pltpu.VMEM((chunks, modes, ROW_BLOCK, width), bf16),
            pltpu.VMEM((chunks, group, held, ROW_BLOCK, width), bf16),
            pltpu.VMEM((steps, outer, kept, width), bf16),
            pltpu.VMEM((steps, outer, kept, width), bf16),
            pltpu.VMEM((steps, outer, kept, width), bf16),
            pltpu.VMEM((chunks, group, held, ROW_BLOCK, width), bf16),
            pltpu.VMEM((steps, kept, width), bf16),
            pltpu.VMEM((kept, width), jnp.float32),
            pltpu.VMEM(fwd.shape[1:], bf16),
            pltpu.VMEM(bwd.shape[1:], bf16),
            pltpu.VMEM(lon.shape, bf16),
            pltpu.VMEM(local.shape, bf16),
            pltpu.VMEM((layers, steps, channels, width), bf16),
            pltpu.VMEM((steps, width, width), bf16),
            pltpu.VMEM((modes * ROW_BLOCK, width), jnp.float32),
            pltpu.VMEM((ROW_BLOCK * channels, 2 * modes), bf16),
            pltpu.VMEM((many, many), bf16),
            dma((chunks,)), dma((5,)), dma((layers, steps)),
            dma((part_count,)), dma((slots,)), dma((2, steps)), dma((2, steps)),
            dma((part_count, group)), dma((part_count, group)),
            dma((steps, outer)), dma((steps, outer)),
            dma((steps, outer)), dma((steps, outer)),
            dma((slots, group)), dma((slots, group)),
        ],
        compiler_params=pltpu.CompilerParams(
            collective_id=0, has_side_effects=True, vmem_limit_bytes=NET_VMEM
        ),
        name="net_part",
    )(*operands)


def field_kernel(y_ref, local_ref, back_ref, out_ref, turned, turn, out_buf, out_sem):
    chunks, modes, rows, width = y_ref.shape
    channels = width // 2
    span = out_buf.shape[1]
    pieces = [(i, first) for i in range(chunks) for first in range(0, rows, span)]

    def out_copy(k):
        i, first = pieces[k]
        return pltpu.make_async_copy(
            out_buf.at[k % 2], out_ref.at[pl.ds(i * rows + first, span)], out_sem.at[k % 2]
        )

    for k, (i, first) in enumerate(pieces):
        if first == 0:
            spectrum_block(y_ref[i], turn, turned)
        if k >= 2:
            out_copy(k - 2).wait()
        own = slice(first * channels, (first + span) * channels)
        field_rows(
            0, span, local_ref.at[i, own], out_buf.at[k % 2], back_ref, turned.at[own]
        )
        out_copy(k).start()
    for k in range(max(0, len(pieces) - 2), len(pieces)):
        out_copy(k).wait()


def field_part(y, local, back):
    chunks, modes, rows, width = y.shape
    channels = width // 2
    lon_count = back.shape[1]
    span = max(1, min(rows, 256 // channels))
    vmem = pl.BlockSpec(memory_space=pltpu.VMEM)
    return pl.pallas_call(
        field_kernel,
        out_shape=jax.ShapeDtypeStruct((chunks * rows, channels, lon_count), jnp.bfloat16),
        in_specs=[vmem] * 3,
        out_specs=pl.BlockSpec(memory_space=pltpu.HBM),
        scratch_shapes=[
            pltpu.VMEM((rows * channels, 2 * modes), jnp.bfloat16),
            pltpu.VMEM((modes * rows, width), jnp.float32),
            pltpu.VMEM((2, span, channels, lon_count), jnp.bfloat16),
            pltpu.SemaphoreType.DMA((2,)),
        ],
        compiler_params=pltpu.CompilerParams(vmem_limit_bytes=FIELD_VMEM),
        name="field_part",
    )(y, local, back)


def shards(fields, spectral_weight, local_weight):
    row_count, channels, lon_count = fields.shape
    layer_count, mode_rows = spectral_weight.shape[:2]
    devices = lax.axis_size("lat")
    group = math.gcd(devices, 16)
    table = lon_table(lon_count, mode_rows)
    forward_lon = jnp.asarray(
        (table / math.sqrt(lon_count)).reshape(lon_count, 2 * mode_rows), jnp.bfloat16
    )
    backward_lon = jnp.asarray(
        (table.transpose(1, 2, 0) * (0.5 / math.sqrt(mode_rows))).reshape(
            2 * mode_rows, lon_count
        ),
        jnp.bfloat16,
    )
    forward_all, backward_all = lat_tables(devices, group, row_count, KY)
    forward_lat = jnp.asarray(forward_all, jnp.bfloat16)
    backward_lat = jnp.asarray(backward_all, jnp.bfloat16)
    y, local, back = net_part(
        fields, spectral_weight, forward_lat, backward_lat, forward_lon, backward_lon,
        local_weight, devices, group,
    )
    return field_part(y, local, back)


def solution(mesh):
    return jax.shard_map(
        shards,
        mesh=mesh,
        in_specs=(P(("grp", "lat"), None, None), P(), P()),
        out_specs=P(("grp", "lat"), None, None),
        check_vma=False,
    )
```
